512 devices in a mesh: segment: 2 (over core), lat: 64 (over x, z_lo, y), tok: 4 (over z_hi).
Axes of the slice: x: 4, y: 4, z: 16 (z_hi: 4, z_lo: 4; z = z_hi * 4 + z_lo), core: 2. Of those that a mesh axis runs over, the one named last changes fastest.
Arguments:
- resid_mid: bfloat16 [512, 4608], P('lat', ('segment', 'tok'))
- mlp_out: bfloat16 [512, 4608], P('lat', ('segment', 'tok'))
- post_gain: float32 [4608], P(('segment', 'tok')), may hold values from 0.5 to 1.5
- enc_weight: bfloat16 [4608, 65536], P(('segment', 'tok'), 'lat'), may hold values from -0.09375 to 0.09375
- enc_bias: float32 [65536], P('lat'), may hold values from -3 to 3
- dec_weight: bfloat16 [65536, 4608], P('lat', ('segment', 'tok')), may hold values from -0.046875 to 0.046875
- dec_bias: float32 [4608], P(('segment', 'tok')), may hold values from -3 to 3
- panel_lists: int32 [4, 128], replicated, may hold values from 0 to 511, as said below
Outputs:
- sq_error: float32 [], replicated
- enc_grad: bfloat16 [4608, 65536], P(('segment', 'tok'), 'lat')
- dec_grad: bfloat16 [65536, 4608], P('lat', ('segment', 'tok'))
The draws below stay inside these ranges and needn't reach their ends.
Inputs may be any that keep to these rules, and one draw needn't show every extreme that they name: `panel_lists`: each row lists 128 different panels.
All inputs are finite; a program needn't handle non-finite values.
Results may differ from the reference program's by a relative error of at most 0.014.
Values may be sent and summed in bfloat16 or wider, within the bound.
A program may use at most 64 MiB of HBM per device.

```python
import jax
import jax.numpy as jnp
from jax import lax

D = 4608
PANEL = 128
BLOCK = 128
BLOCKS = 4
LATENTS = 65536
PANELS = 512
K_ACT = 128
TOKENS = 512
N_SEGMENT = 2
N_TOK = 4


def draw_resid_mid(key, part):
    key_values = jax.random.fold_in(key, 11)
    column = jnp.arange(D, dtype=jnp.float32) / D
    values = jax.random.normal(key_values, (TOKENS, D), jnp.float32)
    rate = 2.3
    column_scale = jnp.exp(column * rate) * jnp.sqrt(2.0 * rate / (jnp.exp(2.0 * rate) - 1.0))
    return (values * column_scale[None, :]).astype(jnp.bfloat16)


def draw_mlp_out(key, part):
    key_values, key_rows = jax.random.split(key)
    column = jnp.arange(D, dtype=jnp.float32) / D
    values = jax.random.normal(key_values, (TOKENS, D), jnp.float32)
    column_scale = jnp.exp(column * 2.3)
    row_scale = jnp.exp(jax.random.uniform(key_rows, (TOKENS, 1), jnp.float32, 0.0, 2.3))
    return (values * column_scale[None, :] * row_scale).astype(jnp.bfloat16)


def draw_panel_lists(key, part):
    key_favour, key_base = jax.random.split(jax.random.fold_in(key, 7))
    favour = jax.random.randint(key_favour, (PANELS,), 0, 2) * 700
    base = jax.random.randint(key_base, (BLOCKS, PANELS), 0, 1024)
    panel_range = jnp.arange(PANELS, dtype=jnp.int32)
    ends = (panel_range == 0) | (panel_range == PANELS - 1)
    first_row = jnp.arange(BLOCKS, dtype=jnp.int32)[:, None] == 0
    score = base + favour[None, :] + jnp.where(ends[None, :] & first_row, 4096, 0)
    score = score * PANELS + panel_range[None, :]
    picked = lax.top_k(score, K_ACT)[1]
    return picked.astype(jnp.int32)


def steps_of(stream_key, shape, shards, low, top_value):
    def one(position, shards_of):
        steps = jax.random.uniform(jax.random.fold_in(jax.random.fold_in(stream_key, 6), position), (shards_of,), jnp.float32, low / len(shards), top_value / len(shards))
        return jnp.repeat(jnp.exp(steps), shape[position] // shards_of).reshape((-1,) + (1,) * (len(shape) - position - 1))

    level = one(*shards[0])
    for cut in shards[1:]:
        level = level * one(*cut)
    return level


def scatter_about(rng, shape, scale, reach, pieces=(), kind=jnp.bfloat16):
    loudness = steps_of(rng, shape, pieces, -0.22, 0.18) if pieces else 1.0
    drawn = jax.random.normal(rng, shape, jnp.float32) * scale * loudness
    return jnp.minimum(jnp.maximum(drawn, -reach), reach).astype(kind)


def setup_inputs(seed: int = 0) -> dict:
    seeds = jax.random.split(jax.random.key(seed), 9)
    resid_mid = draw_resid_mid(jax.random.fold_in(seeds[8], 71), 0)
    mlp_out = draw_mlp_out(jax.random.fold_in(seeds[8], 71), 0)
    post_gain = jnp.clip(1.0 + 0.1 * jax.random.normal(seeds[2], (D,), jnp.float32), 0.5, 1.5)
    enc_weight = scatter_about(seeds[3], (D, LATENTS), D ** -0.5, 0.09375, ((0, 8), (1, 64)))
    enc_bias = scatter_about(seeds[4], (LATENTS,), 0.5, 3.0, ((0, 64),), jnp.float32)
    dec_weight = scatter_about(seeds[5], (LATENTS, D), (K_ACT * PANEL) ** -0.5, 0.046875, ((0, 64), (1, 8)))
    dec_bias = scatter_about(seeds[6], (D,), 0.5, 3.0, ((0, 8),), jnp.float32)
    panel_lists = draw_panel_lists(jax.random.fold_in(seeds[8], 71), 0)
    return {"resid_mid": resid_mid, "mlp_out": mlp_out, "post_gain": post_gain, "enc_weight": enc_weight, "enc_bias": enc_bias, "dec_weight": dec_weight, "dec_bias": dec_bias, "panel_lists": panel_lists}


def gelu_pair(preact):
    activation, pullback = jax.vjp(jax.nn.gelu, preact)
    return (activation, pullback(jnp.ones_like(preact))[0])

def rounded(value):
    return lax.optimization_barrier(value.astype(jnp.bfloat16)).astype(jnp.float32)

def reference(resid_mid, mlp_out, post_gain, enc_weight, enc_bias, dec_weight, dec_bias, panel_lists):
    groups = N_SEGMENT * N_TOK
    width = D // groups
    model_rows = mlp_out.astype(jnp.float32)
    mean_square = lax.optimization_barrier(jnp.mean(model_rows * model_rows, axis=1, keepdims=True))
    normed = model_rows * lax.rsqrt(mean_square + 1e-06) * post_gain[None, :]
    features = (resid_mid.astype(jnp.float32) + normed).astype(jnp.bfloat16)
    centered = (features.astype(jnp.float32) - dec_bias[None, :]).astype(jnp.bfloat16)
    preact = jnp.zeros((TOKENS, LATENTS), jnp.float32)
    for group in range(groups):
        part = jnp.dot(centered[:, group * width:(group + 1) * width], enc_weight[group * width:(group + 1) * width, :], preferred_element_type=jnp.float32)
        preact = preact + rounded(part)
    preact = preact + enc_bias[None, :]
    active = jnp.any(panel_lists[:, :, None] == jnp.arange(PANELS, dtype=jnp.int32)[None, None, :], axis=1).astype(jnp.float32)
    tile_mask = jnp.broadcast_to(active[:, None, :, None], (BLOCKS, BLOCK, PANELS, PANEL)).reshape(TOKENS, LATENTS)
    activation, derivative = gelu_pair(preact)
    latents = (activation * tile_mask).astype(jnp.bfloat16)
    rebuilt = jnp.dot(latents, dec_weight, preferred_element_type=jnp.float32) + dec_bias[None, :]
    error = rebuilt - features.astype(jnp.float32)
    sq_error = jnp.sum(error * error) / (TOKENS * D)
    error_bf = error.astype(jnp.bfloat16)
    dec_grad = jnp.dot(latents.T, error_bf, preferred_element_type=jnp.float32).astype(jnp.bfloat16)
    latent_grad = jnp.zeros((TOKENS, LATENTS), jnp.float32)
    for group in range(groups):
        part = jnp.dot(error_bf[:, group * width:(group + 1) * width], dec_weight[:, group * width:(group + 1) * width].T, preferred_element_type=jnp.float32)
        latent_grad = latent_grad + rounded(part)
    pre_grad = (latent_grad * derivative * tile_mask).astype(jnp.bfloat16)
    enc_grad = jnp.dot(centered.T, pre_grad, preferred_element_type=jnp.float32).astype(jnp.bfloat16)
    return (sq_error, enc_grad, dec_grad)
```

```python
import functools

import jax
import jax.numpy as jnp
from jax import lax
from jax.experimental import pallas as pl
from jax.experimental.pallas import tpu as pltpu
from jax.sharding import PartitionSpec as P

MESH = pl.DeviceIdType.MESH
D = 4608
TOKENS = 512
WIDTH = 576
LOCAL = 1024
PANELS = 8
BLOCKS = 4
BLOCK = 128
OWN = 16
STEP = 256
F32 = jnp.float32
BF16 = jnp.bfloat16
COPIES = 128


def gelu_pair(x):
    k = 0.7978845608028654
    x2 = x * x
    t = jnp.tanh(k * (x + 0.044715 * (x2 * x)))
    half = 0.5 * (1.0 + t)
    slope = half + (0.5 * x * (1.0 - t * t)) * (k * (1.0 + 0.134145 * x2))
    return x * half, slope


def nt(a, b):
    return lax.dot_general(a, b, (((1,), (1,)), ((), ())), preferred_element_type=F32)


def tn(a, b):
    return lax.dot_general(a, b, (((0,), (0,)), ((), ())), preferred_element_type=F32)


def kernel(
    slots,
    table,
    resid,
    mlp,
    gain,
    enc_bias,
    dec_bias,
    enc_w_hbm,
    dec_w_hbm,
    sq_out,
    enc_out,
    dec_out,
    enc_w,
    dec_w,
    sq_buf,
    own_rows,
    gather_y,
    feats,
    centered,
    part,
    pair_send,
    pair_recv,
    ring_send,
    ring_recv,
    slope,
    gathered,
    dense,
    decoded,
    block_own,
    xs_send,
    xs_recv,
    zs_send,
    zs_recv,
    ys_send,
    ys_recv,
    sum_buf,
    enc_v,
    dec_v,
    send_sem,
    recv_sem,
    local_sem,
):
    seg = lax.axis_index("segment")
    lat = lax.axis_index("lat")
    tok = lax.axis_index("tok")
    x = lax.div(lat, 16)
    zl = lax.rem(lax.div(lat, 4), 4)
    y = lax.rem(lat, 4)

    def turn(v, k):
        return lax.rem(v + k, 4)

    def xdev(k):
        return (seg, turn(x, k) * 16 + zl * 4 + y, tok)

    def zdev(k):
        return (seg, x * 16 + turn(zl, k) * 4 + y, tok)

    def ydev(k):
        return (seg, x * 16 + zl * 4 + turn(y, k), tok)

    def tdev(k):
        return (seg, lat, turn(tok, k))

    sibling = (1 - seg, lat, tok)
    group = [sibling] + [(s, lat, turn(tok, k)) for k in (1, 2, 3) for s in (seg, 1 - seg)]

    counter = [0]
    started = []

    def send(src, dst, device):
        i = counter[0]
        counter[0] += 1
        copy = pltpu.make_async_remote_copy(
            src_ref=src,
            dst_ref=dst,
            send_sem=send_sem.at[i],
            recv_sem=recv_sem.at[i],
            device_id=device,
            device_id_type=MESH,
        )
        copy.start()
        started.append(copy)
        return copy

    load_enc = pltpu.make_async_copy(enc_w_hbm, enc_w, local_sem.at[0])
    load_dec = pltpu.make_async_copy(dec_w_hbm, dec_w, local_sem.at[1])
    load_enc.start()
    load_dec.start()

    barrier = pltpu.get_barrier_semaphore()
    peers = group + [dev(k) for dev in (xdev, zdev, ydev) for k in (1, 2, 3)]
    for peer in peers:
        pl.semaphore_signal(barrier, inc=1, device_id=peer, device_id_type=MESH)

    rows = mlp[...].astype(F32)
    me = seg * 4 + tok
    sq_buf[0, me] = jnp.broadcast_to(jnp.sum(rows * rows, axis=1, keepdims=True), (8, 128))
    pl.semaphore_wait(barrier, len(peers))

    def group_sum(buf):
        copies = [send(buf.at[me], buf.at[me], peer) for peer in group]
        for copy in copies:
            copy.wait_recv()
        total = buf[0]
        for i in range(1, 8):
            total = total + buf[i]
        return total

    squares = group_sum(sq_buf.at[0])[:, :1]
    scale = lax.rsqrt(squares / D + 1e-06)
    own = (resid[...].astype(F32) + rows * scale * gain[...]).astype(BF16)
    own_rows[...] = own

    def ring_gather(half, v, dev):
        up = [send(half(v, 0), half(v, 0), dev(1))]
        down = [send(half(v, 1), half(v, 1), dev(3))]
        up.append(send(half(v, 1), half(v, 1), dev(1)))
        down.append(send(half(v, 0), half(v, 0), dev(3)))
        before, after = turn(v, 3), turn(v, 1)
        up[0].wait_recv()
        up.append(send(half(before, 0), half(before, 0), dev(1)))
        down[0].wait_recv()
        down.append(send(half(after, 1), half(after, 1), dev(3)))
        return up, down

    def finish(up, down):
        for copy in up[1:] + down[1:]:
            copy.wait_recv()

    def gather_all(chunk, stage, out):
        stage[y] = chunk
        copies = [send(stage.at[y], stage.at[y], ydev(k)) for k in (1, 2, 3)]
        for copy in copies:
            copy.wait_recv()
        base = pl.multiple_of((x * 4 + zl) * 32, 32)
        out[pl.ds(base, 32), :] = stage[...].reshape(32, WIDTH)
        piece = out.at[pl.ds(base, 32)]
        copies = [send(piece, piece, zdev(k)) for k in (1, 2, 3)]
        for copy in copies:
            copy.wait_recv()

        def half(v, h):
            return out.at[pl.ds(pl.multiple_of(v * BLOCK + h * 64, 64), 64)]

        finish(*ring_gather(half, x, xdev))

    gather_all(own, gather_y.at[0], feats.at[0])
    centered[...] = (feats[0].astype(F32) - dec_bias[...]).astype(BF16)

    def expand(a, weight):
        def body(n, carry):
            columns = pl.ds(pl.multiple_of(n * STEP, STEP), STEP)
            out = jnp.dot(a[...], weight[:, columns], preferred_element_type=F32)
            for i in range(STEP // BLOCK):
                piece = out[:, i * BLOCK : (i + 1) * BLOCK]
                part[n * (STEP // BLOCK) + i] = piece.reshape(TOKENS // OWN, OWN, BLOCK)
            return carry

        lax.fori_loop(0, LOCAL // STEP, body, 0)

    def reduce_slots(use, finish_tile, between=None):
        low = slots // 2
        psend, precv = pair_send.at[use], pair_recv.at[use]
        rsend, rrecv = ring_send.at[use], ring_recv.at[use]

        def loop(body, start=0, stop=slots):
            def step(c, carry):
                body(c, table[1, c], table[0, c] * 8)
                return carry

            lax.fori_loop(start, stop, step, 0)

        pair = {}
        for k in (2, 1, 3, 0):
            t = turn(tok, k)

            def to_pair(c, panel, row):
                psend[t, c] = part[panel, row + (1 - seg) * 4 + t].astype(BF16)

            loop(to_pair)
            pair[k] = send(psend.at[t], precv.at[t], sibling)

        def mine(k, c, panel, row):
            t = turn(tok, k)
            return part[panel, row + seg * 4 + t] + precv[t, c].astype(F32)

        pair[2].wait_recv()

        def far(c, panel, row):
            rsend[0, c] = mine(2, c, panel, row).astype(BF16)

        loop(far)
        first_up = send(rsend.at[0, pl.ds(0, low)], rrecv.at[0, pl.ds(0, low)], tdev(1))
        first_down = send(rsend.at[0, pl.ds(low, low)], rrecv.at[0, pl.ds(low, low)], tdev(3))
        pair[1].wait_recv()

        def near_up(c, panel, row):
            rsend[1, c] = mine(1, c, panel, row).astype(BF16)

        loop(near_up, low, slots)
        second_up = send(rsend.at[1, pl.ds(low, low)], rrecv.at[1, pl.ds(low, low)], tdev(1))
        pair[3].wait_recv()

        def near_down(c, panel, row):
            rsend[2, c] = mine(3, c, panel, row).astype(BF16)

        loop(near_down, 0, low)
        second_down = send(rsend.at[2, pl.ds(0, low)], rrecv.at[2, pl.ds(0, low)], tdev(3))

        first_up.wait_recv()

        def merged_up(c, panel, row):
            rsend[1, c] = (mine(1, c, panel, row) + rrecv[0, c].astype(F32)).astype(BF16)

        loop(merged_up, 0, low)
        third_up = send(rsend.at[1, pl.ds(0, low)], rrecv.at[1, pl.ds(0, low)], tdev(1))
        first_down.wait_recv()

        def merged_down(c, panel, row):
            rsend[2, c] = (mine(3, c, panel, row) + rrecv[0, c].astype(F32)).astype(BF16)

        loop(merged_down, low, slots)
        third_down = send(rsend.at[2, pl.ds(low, low)], rrecv.at[2, pl.ds(low, low)], tdev(3))
        pair[0].wait_recv()
        if between is not None:
            between()
        for copy in (second_up, second_down, third_up, third_down):
            copy.wait_recv()
        all_tiles = gathered.at[use]

        def last(c, panel, row):
            total = mine(0, c, panel, row) + rrecv[1, c].astype(F32) + rrecv[2, c].astype(F32)
            all_tiles[me, c] = finish_tile(c, panel, total).astype(BF16)

        loop(last)

        def half(v, h):
            return all_tiles.at[seg * 4 + v, pl.ds(h * low, low)]

        def whole(v):
            return all_tiles.at[seg * 4 + v]

        up, down = ring_gather(half, tok, tdev)
        crossing = [send(whole(tok), whole(tok), sibling)]
        up[1].wait_recv()
        before = turn(tok, 3)
        crossing.append(send(whole(before), whole(before), sibling))
        down[1].wait_recv()
        after = turn(tok, 1)
        crossing.append(send(whole(after), whole(after), sibling))
        up[2].wait_recv()
        down[2].wait_recv()
        far_side = turn(tok, 2)
        crossing.append(send(whole(far_side), whole(far_side), sibling))
        for copy in crossing:
            copy.wait_recv()

        def spread(b, carry):
            for p in range(PANELS):
                slot = table[2, b * PANELS + p]
                active = table[3, b * PANELS + p] > 0
                for j in range(8):
                    tile = all_tiles[j, slot]
                    at = pl.multiple_of(b * BLOCK + j * OWN, OWN)
                    dense[use, pl.ds(at, OWN), p * BLOCK : (p + 1) * BLOCK] = jnp.where(
                        active, tile, jnp.zeros_like(tile)
                    )
            return carry

        lax.fori_loop(0, BLOCKS, spread, 0)

    load_enc.wait()
    expand(centered, enc_w)

    def latents_of(c, panel, total):
        activation, derivative = gelu_pair(total + enc_bias[pl.ds(panel, 1), :])
        slope[c] = derivative
        return activation

    reduce_slots(0, latents_of)

    load_dec.wait()
    latents = dense.at[0]

    def decode_block(k, carry):
        b = pl.multiple_of(turn(x, k) * BLOCK, BLOCK)
        decoded[k] = nt(latents[pl.ds(b, BLOCK), :], dec_w[...])
        return carry

    lax.fori_loop(0, BLOCKS, decode_block, 0)

    def decode(k):
        return decoded[k]

    far = decode(2)
    xs_send[0] = far.astype(BF16)
    first_up = send(xs_send.at[0, pl.ds(0, 64)], xs_recv.at[0, pl.ds(0, 64)], xdev(1))
    first_down = send(xs_send.at[0, pl.ds(64, 64)], xs_recv.at[0, pl.ds(64, 64)], xdev(3))
    near = decode(1)
    xs_send[1, 64:, :] = near[64:, :].astype(BF16)
    second_up = send(xs_send.at[1, pl.ds(64, 64)], xs_recv.at[1, pl.ds(64, 64)], xdev(1))
    block_own[0:64, :] = near[:64, :]
    near = decode(3)
    xs_send[2, :64, :] = near[:64, :].astype(BF16)
    second_down = send(xs_send.at[2, pl.ds(0, 64)], xs_recv.at[2, pl.ds(0, 64)], xdev(3))
    block_own[64:128, :] = near[64:, :]
    first_up.wait_recv()
    xs_send[1, :64, :] = (block_own[0:64, :] + xs_recv[0, :64, :].astype(F32)).astype(BF16)
    third_up = send(xs_send.at[1, pl.ds(0, 64)], xs_recv.at[1, pl.ds(0, 64)], xdev(1))
    first_down.wait_recv()
    xs_send[2, 64:, :] = (block_own[64:128, :] + xs_recv[0, 64:, :].astype(F32)).astype(BF16)
    third_down = send(xs_send.at[2, pl.ds(64, 64)], xs_recv.at[2, pl.ds(64, 64)], xdev(3))
    block_own[...] = decode(0)
    for copy in (second_up, second_down, third_up, third_down):
        copy.wait_recv()
    block_own[...] = block_own[...] + xs_recv[1].astype(F32) + xs_recv[2].astype(F32)

    copies = []
    for k in (1, 2, 3):
        at = pl.multiple_of(turn(zl, k) * 32, 32)
        zs_send[k - 1] = block_own[pl.ds(at, 32), :].astype(BF16)
        copies.append(send(zs_send.at[k - 1], zs_recv.at[k - 1], zdev(k)))
    quarter = block_own[pl.ds(pl.multiple_of(zl * 32, 32), 32), :]
    for k in (1, 2, 3):
        copies[k - 1].wait_recv()
        quarter = quarter + zs_recv[k - 1].astype(F32)
    block_own[0:32, :] = quarter
    copies = []
    for k in (1, 2, 3):
        at = pl.multiple_of(turn(y, k) * 8, 8)
        ys_send[k - 1] = block_own[pl.ds(at, 8), :].astype(BF16)
        copies.append(send(ys_send.at[k - 1], ys_recv.at[k - 1], ydev(k)))
    rebuilt = block_own[pl.ds(pl.multiple_of(y * 8, 8), 8), :]
    for k in (1, 2, 3):
        copies[k - 1].wait_recv()
        rebuilt = rebuilt + ys_recv[k - 1].astype(F32)

    error = rebuilt + dec_bias[...] - own_rows[...].astype(F32)
    gather_all(error.astype(BF16), gather_y.at[1], feats.at[1])
    errors = feats.at[1]

    squared = jnp.sum(error * error, axis=1, keepdims=True)
    squared = jnp.sum(squared, axis=0, keepdims=True)
    loss = jnp.broadcast_to(squared, (8, 128))

    def loss_step(i, v, dev, value):
        sum_buf[i, v] = value
        return [send(sum_buf.at[i, v], sum_buf.at[i, v], dev(k)) for k in (1, 2, 3)]

    def loss_sum(i, copies):
        for copy in copies:
            copy.wait_recv()
        return (sum_buf[i, 0] + sum_buf[i, 1]) + (sum_buf[i, 2] + sum_buf[i, 3])

    expand(errors, dec_w)
    for i, v, dev in ((0, y, ydev), (1, zl, zdev), (2, x, xdev)):
        loss = loss_sum(i, loss_step(i, v, dev, loss))
    sq_buf[1, me] = loss
    sq_out[...] = group_sum(sq_buf.at[1]) / (TOKENS * D)

    store_dec = pltpu.make_async_copy(dec_v, dec_out, local_sem.at[2])
    store_enc = pltpu.make_async_copy(enc_v, enc_out, local_sem.at[3])

    def outer(a, use, result):
        def body(n, carry):
            columns = pl.ds(pl.multiple_of(n * STEP, STEP), STEP)
            result[:, columns] = tn(a[...], dense[use, :, columns]).astype(BF16)
            return carry

        lax.fori_loop(0, LOCAL // STEP, body, 0)

    def decoder_gradient():
        outer(errors, 0, dec_v)
        store_dec.start()

    reduce_slots(1, lambda c, panel, total: total * slope[c], decoder_gradient)
    outer(centered, 1, enc_v)
    store_enc.start()
    store_dec.wait()
    store_enc.wait()
    for copy in started:
        copy.wait_send()


def step(slots, table, resid_mid, mlp_out, post_gain, enc_weight, enc_bias, dec_weight, dec_bias):
    vmem = pl.BlockSpec(memory_space=pltpu.VMEM)
    anywhere = pl.BlockSpec(memory_space=pl.ANY)
    low = pltpu.VMEM
    return pl.pallas_call(
        functools.partial(kernel, slots),
        name="sae_step",
        out_shape=(
            jax.ShapeDtypeStruct((8, 128), F32),
            jax.ShapeDtypeStruct((WIDTH, LOCAL), BF16),
            jax.ShapeDtypeStruct((WIDTH, LOCAL), BF16),
        ),
        in_specs=[pl.BlockSpec(memory_space=pltpu.SMEM)] + [vmem] * 5 + [anywhere] * 2,
        out_specs=(vmem, anywhere, anywhere),
        scratch_shapes=[
            low((WIDTH, LOCAL), BF16),
            low((WIDTH, LOCAL), BF16),
            low((2, 8, 8, 128), F32),
            low((8, WIDTH), BF16),
            low((2, 4, 8, WIDTH), BF16),
            low((2, TOKENS, WIDTH), BF16),
            low((TOKENS, WIDTH), BF16),
            low((PANELS, TOKENS // OWN, OWN, BLOCK), F32),
            low((2, 4, slots, OWN, BLOCK), BF16),
            low((2, 4, slots, OWN, BLOCK), BF16),
            low((2, 3, slots, OWN, BLOCK), BF16),
            low((2, 3, slots, OWN, BLOCK), BF16),
            low((slots, OWN, BLOCK), F32),
            low((2, 8, slots, OWN, BLOCK), BF16),
            low((2, TOKENS, LOCAL), BF16),
            low((BLOCKS, BLOCK, WIDTH), F32),
            low((BLOCK, WIDTH), F32),
            low((3, BLOCK, WIDTH), BF16),
            low((3, BLOCK, WIDTH), BF16),
            low((3, 32, WIDTH), BF16),
            low((3, 32, WIDTH), BF16),
            low((3, 8, WIDTH), BF16),
            low((3, 8, WIDTH), BF16),
            low((3, 4, 8, 128), F32),
            low((WIDTH, LOCAL), BF16),
            low((WIDTH, LOCAL), BF16),
            pltpu.SemaphoreType.DMA((COPIES,)),
            pltpu.SemaphoreType.DMA((COPIES,)),
            pltpu.SemaphoreType.DMA((4,)),
        ],
        compiler_params=pltpu.CompilerParams(
            collective_id=0, has_side_effects=True, vmem_limit_bytes=48 * 1024 * 1024
        ),
    )(
        table,
        resid_mid,
        mlp_out,
        post_gain.reshape(1, WIDTH),
        enc_bias.reshape(PANELS, BLOCK),
        dec_bias.reshape(1, WIDTH),
        enc_weight,
        dec_weight.T,
    )


def tables(panel_lists):
    ids = lax.axis_index("lat") * PANELS + jnp.arange(PANELS, dtype=jnp.int32)
    active = jnp.any(panel_lists[:, :, None] == ids[None, None, :], axis=1).reshape(-1)
    active = active.astype(jnp.int32)
    tiles = jnp.arange(BLOCKS * PANELS, dtype=jnp.int32)
    rank = jnp.sum(jnp.where(tiles[None, :] < tiles[:, None], active[None, :], 0), axis=1)
    here = (rank[None, :] == tiles[:, None]) & (active[None, :] > 0)
    tile = jnp.sum(jnp.where(here, tiles[None, :], 0), axis=1)
    slot = jnp.where(active > 0, rank, 0)
    return jnp.stack([tile // PANELS, tile % PANELS, slot, active]).astype(jnp.int32)


def on_device(
    resid_mid, mlp_out, post_gain, enc_weight, enc_bias, dec_weight, dec_bias, panel_lists
):
    table = tables(panel_lists)
    loss, enc_grad, dec_grad = step(
        32, table, resid_mid, mlp_out, post_gain, enc_weight, enc_bias, dec_weight, dec_bias
    )
    return loss[0, 0], enc_grad, dec_grad.T


def solution(mesh):
    placed = (
        P("lat", ("segment", "tok")),
        P("lat", ("segment", "tok")),
        P(("segment", "tok")),
        P(("segment", "tok"), "lat"),
        P("lat"),
        P("lat", ("segment", "tok")),
        P(("segment", "tok")),
        P(),
    )
    return jax.shard_map(
        on_device,
        mesh=mesh,
        in_specs=placed,
        out_specs=(P(), P(("segment", "tok"), "lat"), P("lat", ("segment", "tok"))),
        check_vma=False,
    )
```

```python
import functools

import jax
import jax.numpy as jnp
from jax import lax
from jax.experimental import pallas as pl
from jax.experimental.pallas import tpu as pltpu
from jax.sharding import PartitionSpec as P

MESH = pl.DeviceIdType.MESH
D = 4608
TOKENS = 512
WIDTH = 576
LOCAL = 1024
PANELS = 8
BLOCKS = 4
BLOCK = 128
OWN = 16
STEP = 256
F32 = jnp.float32
BF16 = jnp.bfloat16
COPIES = 128
CAPACITIES = (16, 20, 32)


def gelu_pair(x):
    k = 0.7978845608028654
    x2 = x * x
    t = jnp.tanh(k * (x + 0.044715 * (x2 * x)))
    half = 0.5 * (1.0 + t)
    slope = half + (0.5 * x * (1.0 - t * t)) * (k * (1.0 + 0.134145 * x2))
    return x * half, slope


def nt(a, b):
    return lax.dot_general(a, b, (((1,), (1,)), ((), ())), preferred_element_type=F32)


def tn(a, b):
    return lax.dot_general(a, b, (((0,), (0,)), ((), ())), preferred_element_type=F32)


def kernel(
    slots,
    table,
    resid_hbm,
    mlp_hbm,
    gain_hbm,
    enc_bias_hbm,
    dec_bias_hbm,
    enc_w_hbm,
    dec_w_hbm,
    sq_out,
    enc_out,
    dec_out,
    resid,
    mlp,
    gain,
    enc_bias,
    dec_bias,
    enc_w,
    dec_w,
    sq_buf,
    own_rows,
    gather_y,
    feats,
    centered,
    part,
    pair_send,
    pair_recv,
    ring_send,
    ring_recv,
    slope,
    gathered,
    dense,
    decoded,
    block_own,
    xs_send,
    xs_recv,
    zs_send,
    zs_recv,
    ys_send,
    ys_recv,
    sum_buf,
    enc_v,
    dec_v,
    send_sem,
    recv_sem,
    local_sem,
):
    seg = lax.axis_index("segment")
    lat = lax.axis_index("lat")
    tok = lax.axis_index("tok")
    x = lax.div(lat, 16)
    zl = lax.rem(lax.div(lat, 4), 4)
    y = lax.rem(lat, 4)

    def turn(v, k):
        return lax.rem(v + k, 4)

    def xdev(k):
        return (seg, turn(x, k) * 16 + zl * 4 + y, tok)

    def zdev(k):
        return (seg, x * 16 + turn(zl, k) * 4 + y, tok)

    def ydev(k):
        return (seg, x * 16 + zl * 4 + turn(y, k), tok)

    def tdev(k):
        return (seg, lat, turn(tok, k))

    sibling = (1 - seg, lat, tok)
    group = [sibling] + [(s, lat, turn(tok, k)) for k in (1, 2, 3) for s in (seg, 1 - seg)]

    counter = [0]
    started = []

    def send(src, dst, device):
        i = counter[0]
        counter[0] += 1
        copy = pltpu.make_async_remote_copy(
            src_ref=src,
            dst_ref=dst,
            send_sem=send_sem.at[i],
            recv_sem=recv_sem.at[i],
            device_id=device,
            device_id_type=MESH,
        )
        copy.start()
        started.append(copy)
        return copy

    loads = [
        pltpu.make_async_copy(src, dst, local_sem.at[i])
        for i, (src, dst) in enumerate(
            (
                (mlp_hbm, mlp),
                (resid_hbm, resid),
                (gain_hbm, gain),
                (enc_bias_hbm, enc_bias),
                (dec_bias_hbm, dec_bias),
                (enc_w_hbm, enc_w),
                (dec_w_hbm, dec_w),
            )
        )
    ]
    for load in loads:
        load.start()

    barrier = pltpu.get_barrier_semaphore()
    peers = group + [dev(k) for dev in (xdev, zdev, ydev) for k in (1, 2, 3)]
    for peer in peers:
        pl.semaphore_signal(barrier, inc=1, device_id=peer, device_id_type=MESH)

    loads[0].wait()
    rows = mlp[...].astype(F32)
    me = seg * 4 + tok
    sq_buf[0, me] = jnp.broadcast_to(jnp.sum(rows * rows, axis=1, keepdims=True), (8, 128))
    pl.semaphore_wait(barrier, len(peers))
    for load in loads[1:]:
        load.wait()

    def group_start(buf):
        return [send(buf.at[me], buf.at[me], peer) for peer in group]

    def group_sum(buf, copies):
        for copy in copies:
            copy.wait_recv()
        total = buf[0]
        for i in range(1, 8):
            total = total + buf[i]
        return total

    squares = group_sum(sq_buf.at[0], group_start(sq_buf.at[0]))[:, :1]
    scale = lax.rsqrt(squares / D + 1e-06)
    own = (resid[...].astype(F32) + rows * scale * gain[...]).astype(BF16)
    own_rows[...] = own

    def ring_gather(half, v, dev):
        up = [send(half(v, 0), half(v, 0), dev(1))]
        down = [send(half(v, 1), half(v, 1), dev(3))]
        up.append(send(half(v, 1), half(v, 1), dev(1)))
        down.append(send(half(v, 0), half(v, 0), dev(3)))
        before, after = turn(v, 3), turn(v, 1)
        up[0].wait_recv()
        up.append(send(half(before, 0), half(before, 0), dev(1)))
        down[0].wait_recv()
        down.append(send(half(after, 1), half(after, 1), dev(3)))
        return up, down

    def gather_all(chunk, stage, out, side=None):
        def side_start(i, v, dev, value):
            if side is None:
                return None
            sum_buf[i, v] = value
            return [send(sum_buf.at[i, v], sum_buf.at[i, v], dev(k)) for k in (1, 2, 3)]

        def side_sum(i, copies):
            if side is None:
                return None
            for copy in copies:
                copy.wait_recv()
            return (sum_buf[i, 0] + sum_buf[i, 1]) + (sum_buf[i, 2] + sum_buf[i, 3])

        stage[y] = chunk
        copies = [send(stage.at[y], stage.at[y], ydev(k)) for k in (1, 2, 3)]
        beside = side_start(0, y, ydev, side)
        for copy in copies:
            copy.wait_recv()
        base = pl.multiple_of((x * 4 + zl) * 32, 32)
        out[pl.ds(base, 32), :] = stage[...].reshape(32, WIDTH)
        piece = out.at[pl.ds(base, 32)]
        copies = [send(piece, piece, zdev(k)) for k in (1, 2, 3)]
        beside = side_start(1, zl, zdev, side_sum(0, beside))
        for copy in copies:
            copy.wait_recv()

        def half(v, h):
            return out.at[pl.ds(pl.multiple_of(v * BLOCK + h * 64, 64), 64)]

        up, down = ring_gather(half, x, xdev)
        beside = side_start(2, x, xdev, side_sum(1, beside))
        for copy in up[1:] + down[1:]:
            copy.wait_recv()
        return side_sum(2, beside)

    gather_all(own, gather_y.at[0], feats.at[0])
    centered[...] = (feats[0].astype(F32) - dec_bias[...]).astype(BF16)

    def expand(a, weight):
        def body(n, carry):
            columns = pl.ds(pl.multiple_of(n * STEP, STEP), STEP)
            out = jnp.dot(a[...], weight[:, columns], preferred_element_type=F32)
            for i in range(STEP // BLOCK):
                piece = out[:, i * BLOCK : (i + 1) * BLOCK]
                part[n * (STEP // BLOCK) + i] = piece.reshape(TOKENS // OWN, OWN, BLOCK)
            return carry

        lax.fori_loop(0, LOCAL // STEP, body, 0)

    def reduce_slots(use, finish_tile, between=None):
        low = slots // 2
        psend, precv = pair_send.at[use], pair_recv.at[use]
        rsend, rrecv = ring_send.at[use], ring_recv.at[use]

        def loop(body, start=0, stop=slots):
            def step(c, carry):
                body(c, table[1, c], table[0, c] * 8)
                return carry

            lax.fori_loop(start, stop, step, 0)

        pair = {}
        for k in (2, 1, 3, 0):
            t = turn(tok, k)

            def to_pair(c, panel, row):
                psend[t, c] = part[panel, row + (1 - seg) * 4 + t].astype(BF16)

            loop(to_pair)
            pair[k] = send(psend.at[t], precv.at[t], sibling)

        def mine(k, c, panel, row):
            t = turn(tok, k)
            return part[panel, row + seg * 4 + t] + precv[t, c].astype(F32)

        pair[2].wait_recv()

        def far(c, panel, row):
            rsend[0, c] = mine(2, c, panel, row).astype(BF16)

        loop(far)
        first_up = send(rsend.at[0, pl.ds(0, low)], rrecv.at[0, pl.ds(0, low)], tdev(1))
        first_down = send(rsend.at[0, pl.ds(low, low)], rrecv.at[0, pl.ds(low, low)], tdev(3))
        pair[1].wait_recv()

        def near_up(c, panel, row):
            rsend[1, c] = mine(1, c, panel, row).astype(BF16)

        loop(near_up, low, slots)
        second_up = send(rsend.at[1, pl.ds(low, low)], rrecv.at[1, pl.ds(low, low)], tdev(1))
        pair[3].wait_recv()

        def near_down(c, panel, row):
            rsend[2, c] = mine(3, c, panel, row).astype(BF16)

        loop(near_down, 0, low)
        second_down = send(rsend.at[2, pl.ds(0, low)], rrecv.at[2, pl.ds(0, low)], tdev(3))

        first_up.wait_recv()

        def merged_up(c, panel, row):
            rsend[1, c] = (mine(1, c, panel, row) + rrecv[0, c].astype(F32)).astype(BF16)

        loop(merged_up, 0, low)
        third_up = send(rsend.at[1, pl.ds(0, low)], rrecv.at[1, pl.ds(0, low)], tdev(1))
        first_down.wait_recv()

        def merged_down(c, panel, row):
            rsend[2, c] = (mine(3, c, panel, row) + rrecv[0, c].astype(F32)).astype(BF16)

        loop(merged_down, low, slots)
        third_down = send(rsend.at[2, pl.ds(low, low)], rrecv.at[2, pl.ds(low, low)], tdev(3))
        pair[0].wait_recv()
        if between is not None:
            between()
        for copy in (second_up, second_down, third_up, third_down):
            copy.wait_recv()
        all_tiles = gathered.at[use]

        def last(c, panel, row):
            total = mine(0, c, panel, row) + rrecv[1, c].astype(F32) + rrecv[2, c].astype(F32)
            all_tiles[me, c] = finish_tile(c, panel, total).astype(BF16)

        loop(last)

        def half(v, h):
            return all_tiles.at[seg * 4 + v, pl.ds(h * low, low)]

        def whole(v):
            return all_tiles.at[seg * 4 + v]

        up, down = ring_gather(half, tok, tdev)
        crossing = [send(whole(tok), whole(tok), sibling)]
        up[1].wait_recv()
        before = turn(tok, 3)
        crossing.append(send(whole(before), whole(before), sibling))
        down[1].wait_recv()
        after = turn(tok, 1)
        crossing.append(send(whole(after), whole(after), sibling))
        up[2].wait_recv()
        down[2].wait_recv()
        far_side = turn(tok, 2)
        crossing.append(send(whole(far_side), whole(far_side), sibling))
        for copy in crossing:
            copy.wait_recv()

        def spread(b, carry):
            for p in range(PANELS):
                slot = table[2, b * PANELS + p]
                active = table[3, b * PANELS + p] > 0
                for j in range(8):
                    tile = all_tiles[j, slot]
                    at = pl.multiple_of(b * BLOCK + j * OWN, OWN)
                    dense[use, pl.ds(at, OWN), p * BLOCK : (p + 1) * BLOCK] = jnp.where(
                        active, tile, jnp.zeros_like(tile)
                    )
            return carry

        lax.fori_loop(0, BLOCKS, spread, 0)

    expand(centered, enc_w)

    def latents_of(c, panel, total):
        activation, derivative = gelu_pair(total + enc_bias[pl.ds(panel, 1), :])
        slope[c] = derivative
        return activation

    reduce_slots(0, latents_of)

    latents = dense.at[0]

    def decode_block(k, carry):
        b = pl.multiple_of(turn(x, k) * BLOCK, BLOCK)
        decoded[k] = nt(latents[pl.ds(b, BLOCK), :], dec_w[...])
        return carry

    lax.fori_loop(0, BLOCKS, decode_block, 0)

    def decode(k):
        return decoded[k]

    far = decode(2)
    xs_send[0] = far.astype(BF16)
    first_up = send(xs_send.at[0, pl.ds(0, 64)], xs_recv.at[0, pl.ds(0, 64)], xdev(1))
    first_down = send(xs_send.at[0, pl.ds(64, 64)], xs_recv.at[0, pl.ds(64, 64)], xdev(3))
    near = decode(1)
    xs_send[1, 64:, :] = near[64:, :].astype(BF16)
    second_up = send(xs_send.at[1, pl.ds(64, 64)], xs_recv.at[1, pl.ds(64, 64)], xdev(1))
    block_own[0:64, :] = near[:64, :]
    near = decode(3)
    xs_send[2, :64, :] = near[:64, :].astype(BF16)
    second_down = send(xs_send.at[2, pl.ds(0, 64)], xs_recv.at[2, pl.ds(0, 64)], xdev(3))
    block_own[64:128, :] = near[64:, :]
    first_up.wait_recv()
    xs_send[1, :64, :] = (block_own[0:64, :] + xs_recv[0, :64, :].astype(F32)).astype(BF16)
    third_up = send(xs_send.at[1, pl.ds(0, 64)], xs_recv.at[1, pl.ds(0, 64)], xdev(1))
    first_down.wait_recv()
    xs_send[2, 64:, :] = (block_own[64:128, :] + xs_recv[0, 64:, :].astype(F32)).astype(BF16)
    third_down = send(xs_send.at[2, pl.ds(64, 64)], xs_recv.at[2, pl.ds(64, 64)], xdev(3))
    block_own[...] = decode(0)
    for copy in (second_up, second_down, third_up, third_down):
        copy.wait_recv()
    block_own[...] = block_own[...] + xs_recv[1].astype(F32) + xs_recv[2].astype(F32)

    copies = []
    for k in (1, 2, 3):
        at = pl.multiple_of(turn(zl, k) * 32, 32)
        zs_send[k - 1] = block_own[pl.ds(at, 32), :].astype(BF16)
        copies.append(send(zs_send.at[k - 1], zs_recv.at[k - 1], zdev(k)))
    quarter = block_own[pl.ds(pl.multiple_of(zl * 32, 32), 32), :]
    for k in (1, 2, 3):
        copies[k - 1].wait_recv()
        quarter = quarter + zs_recv[k - 1].astype(F32)
    block_own[0:32, :] = quarter
    copies = []
    for k in (1, 2, 3):
        at = pl.multiple_of(turn(y, k) * 8, 8)
        ys_send[k - 1] = block_own[pl.ds(at, 8), :].astype(BF16)
        copies.append(send(ys_send.at[k - 1], ys_recv.at[k - 1], ydev(k)))
    rebuilt = block_own[pl.ds(pl.multiple_of(y * 8, 8), 8), :]
    for k in (1, 2, 3):
        copies[k - 1].wait_recv()
        rebuilt = rebuilt + ys_recv[k - 1].astype(F32)

    error = rebuilt + dec_bias[...] - own_rows[...].astype(F32)
    squared = jnp.sum(jnp.sum(error * error, axis=1, keepdims=True), axis=0, keepdims=True)
    loss = gather_all(
        error.astype(BF16), gather_y.at[1], feats.at[1], jnp.broadcast_to(squared, (8, 128))
    )
    errors = feats.at[1]
    sq_buf[1, me] = loss
    loss_copies = group_start(sq_buf.at[1])

    expand(errors, dec_w)
    store_dec = pltpu.make_async_copy(dec_v, dec_out, local_sem.at[7])
    store_enc = pltpu.make_async_copy(enc_v, enc_out, local_sem.at[8])

    def outer(a, use, result):
        def body(n, carry):
            columns = pl.ds(pl.multiple_of(n * STEP, STEP), STEP)
            result[:, columns] = tn(a[...], dense[use, :, columns]).astype(BF16)
            return carry

        lax.fori_loop(0, LOCAL // STEP, body, 0)

    def decoder_gradient():
        outer(errors, 0, dec_v)
        store_dec.start()
        sq_out[...] = group_sum(sq_buf.at[1], loss_copies) / (TOKENS * D)

    reduce_slots(1, lambda c, panel, total: total * slope[c], decoder_gradient)
    outer(centered, 1, enc_v)
    store_enc.start()
    store_dec.wait()
    store_enc.wait()
    for copy in started:
        copy.wait_send()


def step(place, slots, table, resid_mid, mlp_out, post_gain, enc_weight, enc_bias, dec_weight, dec_bias):
    vmem = pl.BlockSpec(memory_space=pltpu.VMEM)
    hbm = pl.BlockSpec(memory_space=pltpu.HBM)
    low = pltpu.VMEM
    return pl.pallas_call(
        functools.partial(kernel, slots),
        name=f"sae_step_{slots}",
        out_shape=(
            jax.ShapeDtypeStruct((8, 128), F32),
            jax.ShapeDtypeStruct((WIDTH, LOCAL), BF16),
            jax.ShapeDtypeStruct((WIDTH, LOCAL), BF16),
        ),
        in_specs=[pl.BlockSpec(memory_space=pltpu.SMEM)] + [hbm] * 7,
        out_specs=(vmem, hbm, hbm),
        scratch_shapes=[
            low((8, WIDTH), BF16),
            low((8, WIDTH), BF16),
            low((1, WIDTH), F32),
            low((PANELS, BLOCK), F32),
            low((1, WIDTH), F32),
            low((WIDTH, LOCAL), BF16),
            low((WIDTH, LOCAL), BF16),
            low((2, 8, 8, 128), F32),
            low((8, WIDTH), BF16),
            low((2, 4, 8, WIDTH), BF16),
            low((2, TOKENS, WIDTH), BF16),
            low((TOKENS, WIDTH), BF16),
            low((PANELS, TOKENS // OWN, OWN, BLOCK), F32),
            low((2, 4, slots, OWN, BLOCK), BF16),
            low((2, 4, slots, OWN, BLOCK), BF16),
            low((2, 3, slots, OWN, BLOCK), BF16),
            low((2, 3, slots, OWN, BLOCK), BF16),
            low((slots, OWN, BLOCK), F32),
            low((2, 8, slots, OWN, BLOCK), BF16),
            low((2, TOKENS, LOCAL), BF16),
            low((BLOCKS, BLOCK, WIDTH), F32),
            low((BLOCK, WIDTH), F32),
            low((3, BLOCK, WIDTH), BF16),
            low((3, BLOCK, WIDTH), BF16),
            low((3, 32, WIDTH), BF16),
            low((3, 32, WIDTH), BF16),
            low((3, 8, WIDTH), BF16),
            low((3, 8, WIDTH), BF16),
            low((3, 4, 8, 128), F32),
            low((WIDTH, LOCAL), BF16),
            low((WIDTH, LOCAL), BF16),
            pltpu.SemaphoreType.DMA((COPIES,)),
            pltpu.SemaphoreType.DMA((COPIES,)),
            pltpu.SemaphoreType.DMA((9,)),
        ],
        compiler_params=pltpu.CompilerParams(
            collective_id=place, has_side_effects=True, vmem_limit_bytes=48 * 1024 * 1024
        ),
    )(
        table,
        resid_mid,
        mlp_out,
        post_gain.reshape(1, WIDTH),
        enc_bias.reshape(PANELS, BLOCK),
        dec_bias.reshape(1, WIDTH),
        enc_weight,
        dec_weight.T,
    )


def tables(panel_lists):
    ids = lax.axis_index("lat") * PANELS + jnp.arange(PANELS, dtype=jnp.int32)
    active = jnp.any(panel_lists[:, :, None] == ids[None, None, :], axis=1).reshape(-1)
    active = active.astype(jnp.int32)
    tiles = jnp.arange(BLOCKS * PANELS, dtype=jnp.int32)
    rank = jnp.sum(jnp.where(tiles[None, :] < tiles[:, None], active[None, :], 0), axis=1)
    here = (rank[None, :] == tiles[:, None]) & (active[None, :] > 0)
    tile = jnp.sum(jnp.where(here, tiles[None, :], 0), axis=1)
    slot = jnp.where(active > 0, rank, 0)
    return jnp.stack([tile // PANELS, tile % PANELS, slot, active]).astype(jnp.int32)


def on_device(
    resid_mid, mlp_out, post_gain, enc_weight, enc_bias, dec_weight, dec_bias, panel_lists
):
    table = tables(panel_lists)
    groups = jnp.arange(lax.axis_size("lat"), dtype=jnp.int32)
    per_group = jnp.sum(panel_lists.reshape(1, -1) // PANELS == groups[:, None], axis=1)
    most = jnp.max(per_group)
    loss, enc_grad, dec_grad = lax.switch(
        sum((most > slots).astype(jnp.int32) for slots in CAPACITIES[:-1]),
        [functools.partial(step, i, slots) for i, slots in enumerate(CAPACITIES)],
        table,
        resid_mid,
        mlp_out,
        post_gain,
        enc_weight,
        enc_bias,
        dec_weight,
        dec_bias,
    )
    return loss[0, 0], enc_grad, dec_grad.T


def solution(mesh):
    placed = (
        P("lat", ("segment", "tok")),
        P("lat", ("segment", "tok")),
        P(("segment", "tok")),
        P(("segment", "tok"), "lat"),
        P("lat"),
        P("lat", ("segment", "tok")),
        P(("segment", "tok")),
        P(),
    )
    return jax.shard_map(
        on_device,
        mesh=mesh,
        in_specs=placed,
        out_specs=(P(), P(("segment", "tok"), "lat"), P("lat", ("segment", "tok"))),
        check_vma=False,
    )
```

```python
import functools

import jax
import jax.numpy as jnp
from jax import lax
from jax.experimental import pallas as pl
from jax.experimental.pallas import tpu as pltpu
from jax.sharding import PartitionSpec as P

MESH = pl.DeviceIdType.MESH
D = 4608
TOKENS = 512
WIDTH = 576
LOCAL = 1024
PANELS = 8
BLOCKS = 4
BLOCK = 128
OWN = 16
STEP = 256
F32 = jnp.float32
BF16 = jnp.bfloat16
COPIES = 192
CAPACITIES = (20, 32)


def gelu_pair(x):
    k = 0.7978845608028654
    x2 = x * x
    t = jnp.tanh(k * (x + 0.044715 * (x2 * x)))
    half = 0.5 * (1.0 + t)
    slope = half + (0.5 * x * (1.0 - t * t)) * (k * (1.0 + 0.134145 * x2))
    return x * half, slope


def nt(a, b):
    return lax.dot_general(a, b, (((1,), (1,)), ((), ())), preferred_element_type=F32)


def tn(a, b):
    return lax.dot_general(a, b, (((0,), (0,)), ((), ())), preferred_element_type=F32)


def kernel(
    slots,
    table,
    resid_hbm,
    mlp_hbm,
    gain_hbm,
    enc_bias_hbm,
    dec_bias_hbm,
    enc_w_hbm,
    dec_w_hbm,
    sq_out,
    enc_out,
    dec_out,
    resid,
    mlp,
    gain,
    enc_bias,
    dec_bias,
    enc_w,
    dec_w,
    sq_buf,
    own_rows,
    gather_y,
    feats,
    centered,
    part,
    pair_send,
    pair_recv,
    ring_send,
    ring_recv,
    slope,
    gathered,
    dense,
    decoded,
    block_own,
    xs_send,
    xs_recv,
    ps_send,
    ps_recv,
    sum_buf,
    enc_v,
    dec_v,
    send_sem,
    recv_sem,
    local_sem,
):
    seg = lax.axis_index("segment")
    lat = lax.axis_index("lat")
    tok = lax.axis_index("tok")
    x = lax.div(lat, 16)
    zl = lax.rem(lax.div(lat, 4), 4)
    y = lax.rem(lat, 4)

    def turn(v, k):
        return lax.rem(v + k, 4)

    def xdev(k):
        return (seg, turn(x, k) * 16 + zl * 4 + y, tok)

    def plane(i, j):
        return turn(zl, i) * 4 + turn(y, j)

    near = [(i, j) for i in range(4) for j in range(4) if i or j]
    spot = zl * 4 + y

    def ydev(k):
        return pdev(0, k)

    def zdev(k):
        return pdev(k, 0)

    def pdev(i, j):
        return (seg, x * 16 + plane(i, j), tok)

    def tdev(k):
        return (seg, lat, turn(tok, k))

    sibling = (1 - seg, lat, tok)
    group = [sibling] + [(s, lat, turn(tok, k)) for k in (1, 2, 3) for s in (seg, 1 - seg)]

    counter = [0]
    started = []

    def send(src, dst, device):
        i = counter[0]
        counter[0] += 1
        copy = pltpu.make_async_remote_copy(
            src_ref=src,
            dst_ref=dst,
            send_sem=send_sem.at[i],
            recv_sem=recv_sem.at[i],
            device_id=device,
            device_id_type=MESH,
        )
        copy.start()
        started.append(copy)
        return copy

    loads = [
        pltpu.make_async_copy(src, dst, local_sem.at[i])
        for i, (src, dst) in enumerate(
            (
                (mlp_hbm, mlp),
                (resid_hbm, resid),
                (gain_hbm, gain),
                (enc_bias_hbm, enc_bias),
                (dec_bias_hbm, dec_bias),
                (enc_w_hbm, enc_w),
                (dec_w_hbm, dec_w),
            )
        )
    ]
    for load in loads:
        load.start()

    barrier = pltpu.get_barrier_semaphore()
    peers = group + [xdev(k) for k in (1, 2, 3)] + [pdev(i, j) for i, j in near]
    for peer in peers:
        pl.semaphore_signal(barrier, inc=1, device_id=peer, device_id_type=MESH)

    loads[0].wait()
    rows = mlp[...].astype(F32)
    me = seg * 4 + tok
    sq_buf[0, me] = jnp.broadcast_to(jnp.sum(rows * rows, axis=1, keepdims=True), (8, 128))
    pl.semaphore_wait(barrier, len(peers))
    for load in loads[1:7]:
        load.wait()

    def group_start(buf):
        return [send(buf.at[me], buf.at[me], peer) for peer in group]

    def group_sum(buf, copies):
        for copy in copies:
            copy.wait_recv()
        total = buf[0]
        for i in range(1, 8):
            total = total + buf[i]
        return total

    squares = group_sum(sq_buf.at[0], group_start(sq_buf.at[0]))[:, :1]
    scale = lax.rsqrt(squares / D + 1e-06)
    own = (resid[...].astype(F32) + rows * scale * gain[...]).astype(BF16)
    own_rows[...] = own

    def ring_gather(piece, cuts, v, dev):
        a, b, c, d = cuts

        def pass_on(owner, start, stop, k):
            ref = piece(owner, start, stop)
            return send(ref, ref, dev(k))

        up = [pass_on(v, 0, a, 1), pass_on(v, a, b, 1)]
        down = [pass_on(v, b, c, 3), pass_on(v, c, d, 3)]
        up.append(pass_on(v, b, d, 1))
        down.append(pass_on(v, 0, b, 3))
        before, after = turn(v, 3), turn(v, 1)
        for i, low, high in ((0, (0, a), (b, c)), (1, (a, b), (c, d))):
            up[i].wait_recv()
            up.append(pass_on(before, *low, 1))
            down[i].wait_recv()
            down.append(pass_on(after, *high, 3))
        return up, down

    def gather_all(chunk, stage, out, side=None):
        def side_start(i, v, dev, value):
            if side is None:
                return None
            sum_buf[i, v] = value
            return [send(sum_buf.at[i, v], sum_buf.at[i, v], dev(k)) for k in (1, 2, 3)]

        def side_sum(i, copies):
            if side is None:
                return None
            for copy in copies:
                copy.wait_recv()
            return (sum_buf[i, 0] + sum_buf[i, 1]) + (sum_buf[i, 2] + sum_buf[i, 3])

        stage[spot] = chunk
        copies = [send(stage.at[spot], stage.at[spot], pdev(i, j)) for i, j in near]
        beside = side_start(0, y, ydev, side)
        for copy in copies:
            copy.wait_recv()
        out[pl.ds(pl.multiple_of(x * BLOCK, BLOCK), BLOCK), :] = stage[...].reshape(BLOCK, WIDTH)

        def piece(v, start, stop):
            return out.at[pl.ds(pl.multiple_of(v * BLOCK + start, 32), stop - start)]

        up, down = ring_gather(piece, (32, 64, 96, 128), x, xdev)
        beside = side_start(1, zl, zdev, side_sum(0, beside))
        for copy in up[2:] + down[2:]:
            copy.wait_recv()
        return side_start(2, x, xdev, side_sum(1, beside)), side_sum

    gather_all(own, gather_y.at[0], feats.at[0])
    centered[...] = (feats[0].astype(F32) - dec_bias[...]).astype(BF16)

    def expand(a, weight):
        def body(n, carry):
            columns = pl.ds(pl.multiple_of(n * STEP, STEP), STEP)
            out = jnp.dot(a[...], weight[:, columns], preferred_element_type=F32)
            for i in range(STEP // BLOCK):
                piece = out[:, i * BLOCK : (i + 1) * BLOCK]
                part[n * (STEP // BLOCK) + i] = piece.reshape(TOKENS // OWN, OWN, BLOCK)
            return carry

        lax.fori_loop(0, LOCAL // STEP, body, 0)

    def reduce_slots(use, finish_tile, between=None):
        low = slots // 2
        psend, precv = pair_send.at[use], pair_recv.at[use]
        rsend, rrecv = ring_send.at[use], ring_recv.at[use]

        def loop(body, start=0, stop=slots):
            def step(c, carry):
                body(c, table[1, c], table[0, c] * 8)
                return carry

            lax.fori_loop(start, stop, step, 0)

        pair = {}
        for k in (2, 1, 3, 0):
            t = turn(tok, k)

            def to_pair(c, panel, row):
                psend[t, c] = part[panel, row + (1 - seg) * 4 + t].astype(BF16)

            loop(to_pair)
            pair[k] = send(psend.at[t], precv.at[t], sibling)

        def mine(k, c, panel, row):
            t = turn(tok, k)
            return part[panel, row + seg * 4 + t] + precv[t, c].astype(F32)

        pair[2].wait_recv()

        def far(c, panel, row):
            rsend[0, c] = mine(2, c, panel, row).astype(BF16)

        def ring(i, start, stop, k):
            span = pl.ds(start, stop - start)
            return send(rsend.at[i, span], rrecv.at[i, span], tdev(k))

        quarter = low // 2
        lows = ((0, quarter), (quarter, low))
        highs = ((low, low + quarter), (low + quarter, slots))
        first_up, first_down = [], []
        for i in (0, 1):
            loop(far, *lows[i])
            first_up.append(ring(0, *lows[i], 1))
            loop(far, *highs[i])
            first_down.append(ring(0, *highs[i], 3))
        pair[1].wait_recv()

        def near_up(c, panel, row):
            rsend[1, c] = mine(1, c, panel, row).astype(BF16)

        loop(near_up, low, slots)
        rest = [ring(1, low, slots, 1)]
        pair[3].wait_recv()

        def near_down(c, panel, row):
            rsend[2, c] = mine(3, c, panel, row).astype(BF16)

        loop(near_down, 0, low)
        rest.append(ring(2, 0, low, 3))

        def merged_up(c, panel, row):
            rsend[1, c] = (mine(1, c, panel, row) + rrecv[0, c].astype(F32)).astype(BF16)

        def merged_down(c, panel, row):
            rsend[2, c] = (mine(3, c, panel, row) + rrecv[0, c].astype(F32)).astype(BF16)

        for i in (0, 1):
            first_up[i].wait_recv()
            loop(merged_up, *lows[i])
            rest.append(ring(1, *lows[i], 1))
            first_down[i].wait_recv()
            loop(merged_down, *highs[i])
            rest.append(ring(2, *highs[i], 3))
        pair[0].wait_recv()
        if between is not None:
            between()
        for copy in rest:
            copy.wait_recv()
        all_tiles = gathered.at[use]

        def last(c, panel, row):
            total = mine(0, c, panel, row) + rrecv[1, c].astype(F32) + rrecv[2, c].astype(F32)
            all_tiles[me, c] = finish_tile(c, panel, total).astype(BF16)

        loop(last)

        def piece(v, start, stop):
            return all_tiles.at[seg * 4 + v, pl.ds(start, stop - start)]

        def whole(v):
            return all_tiles.at[seg * 4 + v]

        crossing = [send(whole(tok), whole(tok), sibling)]
        up, down = ring_gather(piece, (quarter, low, low + quarter, slots), tok, tdev)
        up[2].wait_recv()
        before = turn(tok, 3)
        crossing.append(send(whole(before), whole(before), sibling))
        down[2].wait_recv()
        after = turn(tok, 1)
        crossing.append(send(whole(after), whole(after), sibling))
        for copy in up[3:] + down[3:]:
            copy.wait_recv()
        far_side = turn(tok, 2)
        crossing.append(send(whole(far_side), whole(far_side), sibling))
        for copy in crossing:
            copy.wait_recv()

        def spread(b, carry):
            for p in range(PANELS):
                slot = table[2, b * PANELS + p]
                active = table[3, b * PANELS + p] > 0
                for j in range(8):
                    tile = all_tiles[j, slot]
                    at = pl.multiple_of(b * BLOCK + j * OWN, OWN)
                    dense[use, pl.ds(at, OWN), p * BLOCK : (p + 1) * BLOCK] = jnp.where(
                        active, tile, jnp.zeros_like(tile)
                    )
            return carry

        lax.fori_loop(0, BLOCKS, spread, 0)

    expand(centered, enc_w)

    def latents_of(c, panel, total):
        activation, derivative = gelu_pair(total + enc_bias[pl.ds(panel, 1), :])
        slope[c] = derivative
        return activation

    reduce_slots(0, latents_of)

    latents = dense.at[0]

    def decode_block(k):
        b = pl.multiple_of(turn(x, k) * BLOCK, BLOCK)
        return nt(latents[pl.ds(b, BLOCK), :], dec_w[...])

    far = decode_block(2)
    xs_send[0] = far.astype(BF16)
    first_up = send(xs_send.at[0, pl.ds(0, 64)], xs_recv.at[0, pl.ds(0, 64)], xdev(1))
    first_down = send(xs_send.at[0, pl.ds(64, 64)], xs_recv.at[0, pl.ds(64, 64)], xdev(3))

    def decode_near(i, carry):
        k = turn(i, 3)
        decoded[k] = decode_block(k)
        return carry

    lax.fori_loop(0, 3, decode_near, 0)
    part_up = decoded[1]
    xs_send[1, 64:, :] = part_up[64:, :].astype(BF16)
    second_up = send(xs_send.at[1, pl.ds(64, 64)], xs_recv.at[1, pl.ds(64, 64)], xdev(1))
    block_own[0:64, :] = part_up[:64, :]
    part_down = decoded[3]
    xs_send[2, :64, :] = part_down[:64, :].astype(BF16)
    second_down = send(xs_send.at[2, pl.ds(0, 64)], xs_recv.at[2, pl.ds(0, 64)], xdev(3))
    block_own[64:128, :] = part_down[64:, :]
    first_up.wait_recv()
    xs_send[1, :64, :] = (block_own[0:64, :] + xs_recv[0, :64, :].astype(F32)).astype(BF16)
    third_up = send(xs_send.at[1, pl.ds(0, 64)], xs_recv.at[1, pl.ds(0, 64)], xdev(1))
    first_down.wait_recv()
    xs_send[2, 64:, :] = (block_own[64:128, :] + xs_recv[0, 64:, :].astype(F32)).astype(BF16)
    third_down = send(xs_send.at[2, pl.ds(64, 64)], xs_recv.at[2, pl.ds(64, 64)], xdev(3))
    block_own[...] = decoded[0]
    for copy in (second_up, second_down, third_up, third_down):
        copy.wait_recv()
    block_own[...] = block_own[...] + xs_recv[1].astype(F32) + xs_recv[2].astype(F32)

    ps_send[...] = block_own[...].astype(BF16).reshape(16, 8, WIDTH)
    copies = [send(ps_send.at[plane(i, j)], ps_recv.at[spot], pdev(i, j)) for i, j in near]
    rebuilt = block_own[pl.ds(pl.multiple_of(spot * 8, 8), 8), :]
    for copy in copies:
        copy.wait_recv()
    for i, j in near:
        rebuilt = rebuilt + ps_recv[plane(i, j)].astype(F32)

    error = rebuilt + dec_bias[...] - own_rows[...].astype(F32)
    squared = jnp.sum(jnp.sum(error * error, axis=1, keepdims=True), axis=0, keepdims=True)
    beside, side_sum = gather_all(
        error.astype(BF16), gather_y.at[1], feats.at[1], jnp.broadcast_to(squared, (8, 128))
    )
    errors = feats.at[1]
    expand(errors, dec_w)
    sq_buf[1, me] = side_sum(2, beside)
    loss_copies = group_start(sq_buf.at[1])
    store_dec = pltpu.make_async_copy(dec_v, dec_out, local_sem.at[7])
    store_enc = pltpu.make_async_copy(enc_v, enc_out, local_sem.at[8])

    def outer(a, use, result):
        def body(n, carry):
            columns = pl.ds(pl.multiple_of(n * STEP, STEP), STEP)
            result[:, columns] = tn(a[...], dense[use, :, columns]).astype(BF16)
            return carry

        lax.fori_loop(0, LOCAL // STEP, body, 0)

    def decoder_gradient():
        outer(errors, 0, dec_v)
        store_dec.start()
        sq_out[...] = group_sum(sq_buf.at[1], loss_copies) / (TOKENS * D)

    reduce_slots(1, lambda c, panel, total: total * slope[c], decoder_gradient)
    outer(centered, 1, enc_v)
    store_enc.start()
    store_dec.wait()
    store_enc.wait()
    for copy in started:
        copy.wait_send()


def step(place, slots, table, resid_mid, mlp_out, post_gain, enc_weight, enc_bias, dec_weight, dec_bias):
    vmem = pl.BlockSpec(memory_space=pltpu.VMEM)
    hbm = pl.BlockSpec(memory_space=pltpu.HBM)
    low = pltpu.VMEM
    return pl.pallas_call(
        functools.partial(kernel, slots),
        name=f"sae_step_{slots}",
        out_shape=(
            jax.ShapeDtypeStruct((8, 128), F32),
            jax.ShapeDtypeStruct((WIDTH, LOCAL), BF16),
            jax.ShapeDtypeStruct((WIDTH, LOCAL), BF16),
        ),
        in_specs=[pl.BlockSpec(memory_space=pltpu.SMEM)] + [hbm] * 7,
        out_specs=(vmem, hbm, hbm),
        scratch_shapes=[
            low((8, WIDTH), BF16),
            low((8, WIDTH), BF16),
            low((1, WIDTH), F32),
            low((PANELS, BLOCK), F32),
            low((1, WIDTH), F32),
            low((WIDTH, LOCAL), BF16),
            low((WIDTH, LOCAL), BF16),
            low((2, 8, 8, 128), F32),
            low((8, WIDTH), BF16),
            low((2, 16, 8, WIDTH), BF16),
            low((2, TOKENS, WIDTH), BF16),
            low((TOKENS, WIDTH), BF16),
            low((PANELS, TOKENS // OWN, OWN, BLOCK), F32),
            low((2, 4, slots, OWN, BLOCK), BF16),
            low((2, 4, slots, OWN, BLOCK), BF16),
            low((2, 3, slots, OWN, BLOCK), BF16),
            low((2, 3, slots, OWN, BLOCK), BF16),
            low((slots, OWN, BLOCK), F32),
            low((2, 8, slots, OWN, BLOCK), BF16),
            low((2, TOKENS, LOCAL), BF16),
            low((BLOCKS, BLOCK, WIDTH), F32),
            low((BLOCK, WIDTH), F32),
            low((3, BLOCK, WIDTH), BF16),
            low((3, BLOCK, WIDTH), BF16),
            low((16, 8, WIDTH), BF16),
            low((16, 8, WIDTH), BF16),
            low((3, 4, 8, 128), F32),
            low((WIDTH, LOCAL), BF16),
            low((WIDTH, LOCAL), BF16),
            pltpu.SemaphoreType.DMA((COPIES,)),
            pltpu.SemaphoreType.DMA((COPIES,)),
            pltpu.SemaphoreType.DMA((9,)),
        ],
        compiler_params=pltpu.CompilerParams(
            collective_id=place, has_side_effects=True, vmem_limit_bytes=48 * 1024 * 1024
        ),
    )(
        table,
        resid_mid,
        mlp_out,
        post_gain.reshape(1, WIDTH),
        enc_bias.reshape(PANELS, BLOCK),
        dec_bias.reshape(1, WIDTH),
        enc_weight,
        dec_weight.T,
    )


def tables(panel_lists):
    ids = lax.axis_index("lat") * PANELS + jnp.arange(PANELS, dtype=jnp.int32)
    active = jnp.any(panel_lists[:, :, None] == ids[None, None, :], axis=1).reshape(-1)
    active = active.astype(jnp.int32)
    tiles = jnp.arange(BLOCKS * PANELS, dtype=jnp.int32)
    rank = jnp.sum(jnp.where(tiles[None, :] < tiles[:, None], active[None, :], 0), axis=1)
    here = (rank[None, :] == tiles[:, None]) & (active[None, :] > 0)
    tile = jnp.sum(jnp.where(here, tiles[None, :], 0), axis=1)
    slot = jnp.where(active > 0, rank, 0)
    return jnp.stack([tile // PANELS, tile % PANELS, slot, active]).astype(jnp.int32)


def on_device(
    resid_mid, mlp_out, post_gain, enc_weight, enc_bias, dec_weight, dec_bias, panel_lists
):
    table = tables(panel_lists)
    groups = jnp.arange(lax.axis_size("lat"), dtype=jnp.int32)
    per_group = jnp.sum(panel_lists.reshape(1, -1) // PANELS == groups[:, None], axis=1)
    most = jnp.max(per_group)
    loss, enc_grad, dec_grad = lax.switch(
        sum((most > slots).astype(jnp.int32) for slots in CAPACITIES[:-1]),
        [functools.partial(step, i, slots) for i, slots in enumerate(CAPACITIES)],
        table,
        resid_mid,
        mlp_out,
        post_gain,
        enc_weight,
        enc_bias,
        dec_weight,
        dec_bias,
    )
    return loss[0, 0], enc_grad, dec_grad.T


def solution(mesh):
    placed = (
        P("lat", ("segment", "tok")),
        P("lat", ("segment", "tok")),
        P(("segment", "tok")),
        P(("segment", "tok"), "lat"),
        P("lat"),
        P("lat", ("segment", "tok")),
        P(("segment", "tok")),
        P(),
    )
    return jax.shard_map(
        on_device,
        mesh=mesh,
        in_specs=placed,
        out_specs=(P(), P(("segment", "tok"), "lat"), P("lat", ("segment", "tok"))),
        check_vma=False,
    )
```

```python
import functools

import jax
import jax.numpy as jnp
from jax import lax
from jax.experimental import pallas as pl
from jax.experimental.pallas import tpu as pltpu
from jax.sharding import PartitionSpec as P

MESH = pl.DeviceIdType.MESH
D = 4608
TOKENS = 512
WIDTH = 576
LOCAL = 1024
PANELS = 8
BLOCKS = 4
BLOCK = 128
OWN = 16
STEP = 256
F32 = jnp.float32
BF16 = jnp.bfloat16
COPIES = 192
CAPACITIES = (16, 20, 32)


def gelu_pair(x):
    k = 0.7978845608028654
    x2 = x * x
    t = jnp.tanh(k * (x + 0.044715 * (x2 * x)))
    half = 0.5 * (1.0 + t)
    slope = half + (0.5 * x * (1.0 - t * t)) * (k * (1.0 + 0.134145 * x2))
    return x * half, slope


def nt(a, b):
    return lax.dot_general(a, b, (((1,), (1,)), ((), ())), preferred_element_type=F32)


def tn(a, b):
    return lax.dot_general(a, b, (((0,), (0,)), ((), ())), preferred_element_type=F32)


def kernel(
    slots,
    table,
    resid_hbm,
    mlp_hbm,
    gain_hbm,
    enc_bias_hbm,
    dec_bias_hbm,
    enc_w_hbm,
    dec_w_hbm,
    sq_out,
    enc_out,
    dec_out,
    resid,
    mlp,
    gain,
    enc_bias,
    dec_bias,
    enc_w,
    dec_w,
    sq_buf,
    own_rows,
    gather_y,
    feats,
    centered,
    part,
    pair_send,
    pair_recv,
    ring_send,
    ring_recv,
    slope,
    gathered,
    dense,
    decoded,
    block_own,
    xs_send,
    xs_recv,
    ps_send,
    ps_recv,
    sum_buf,
    enc_v,
    dec_v,
    send_sem,
    recv_sem,
    local_sem,
):
    seg = lax.axis_index("segment")
    lat = lax.axis_index("lat")
    tok = lax.axis_index("tok")
    x = lax.div(lat, 16)
    zl = lax.rem(lax.div(lat, 4), 4)
    y = lax.rem(lat, 4)

    def turn(v, k):
        return lax.rem(v + k, 4)

    def xdev(k):
        return (seg, turn(x, k) * 16 + zl * 4 + y, tok)

    def plane(i, j):
        return turn(zl, i) * 4 + turn(y, j)

    near = [(i, j) for i in range(4) for j in range(4) if i or j]
    spot = zl * 4 + y

    def ydev(k):
        return pdev(0, k)

    def zdev(k):
        return pdev(k, 0)

    def pdev(i, j):
        return (seg, x * 16 + plane(i, j), tok)

    def tdev(k):
        return (seg, lat, turn(tok, k))

    sibling = (1 - seg, lat, tok)
    group = [sibling] + [(s, lat, turn(tok, k)) for k in (1, 2, 3) for s in (seg, 1 - seg)]

    counter = [0]
    started = []

    def send(src, dst, device):
        i = counter[0]
        counter[0] += 1
        copy = pltpu.make_async_remote_copy(
            src_ref=src,
            dst_ref=dst,
            send_sem=send_sem.at[i],
            recv_sem=recv_sem.at[i],
            device_id=device,
            device_id_type=MESH,
        )
        copy.start()
        started.append(copy)
        return copy

    loads = [
        pltpu.make_async_copy(src, dst, local_sem.at[i])
        for i, (src, dst) in enumerate(
            (
                (mlp_hbm, mlp),
                (resid_hbm, resid),
                (gain_hbm, gain),
                (enc_bias_hbm, enc_bias),
                (dec_bias_hbm, dec_bias),
                (enc_w_hbm, enc_w),
                (dec_w_hbm, dec_w),
            )
        )
    ]
    for load in loads:
        load.start()

    barrier = pltpu.get_barrier_semaphore()
    peers = group + [xdev(k) for k in (1, 2, 3)] + [pdev(i, j) for i, j in near]
    for peer in peers:
        pl.semaphore_signal(barrier, inc=1, device_id=peer, device_id_type=MESH)

    loads[0].wait()
    rows = mlp[...].astype(F32)
    me = seg * 4 + tok
    sq_buf[0, me] = jnp.broadcast_to(jnp.sum(rows * rows, axis=1, keepdims=True), (8, 128))
    pl.semaphore_wait(barrier, len(peers))
    for load in loads[1:7]:
        load.wait()

    def group_start(buf):
        return [send(buf.at[me], buf.at[me], peer) for peer in group]

    def group_sum(buf, copies):
        for copy in copies:
            copy.wait_recv()
        total = buf[0]
        for i in range(1, 8):
            total = total + buf[i]
        return total

    squares = group_sum(sq_buf.at[0], group_start(sq_buf.at[0]))[:, :1]
    scale = lax.rsqrt(squares / D + 1e-06)
    own = (resid[...].astype(F32) + rows * scale * gain[...]).astype(BF16)
    own_rows[...] = own

    def ring_gather(piece, cuts, v, dev):
        a, b, c, d = cuts

        def pass_on(owner, start, stop, k):
            ref = piece(owner, start, stop)
            return send(ref, ref, dev(k))

        up = [pass_on(v, 0, a, 1), pass_on(v, a, b, 1)]
        down = [pass_on(v, b, c, 3), pass_on(v, c, d, 3)]
        up.append(pass_on(v, b, d, 1))
        down.append(pass_on(v, 0, b, 3))
        before, after = turn(v, 3), turn(v, 1)
        for i, low, high in ((0, (0, a), (b, c)), (1, (a, b), (c, d))):
            up[i].wait_recv()
            up.append(pass_on(before, *low, 1))
            down[i].wait_recv()
            down.append(pass_on(after, *high, 3))
        return up, down

    def gather_all(chunk, stage, out, side=None):
        def side_start(i, v, dev, value):
            if side is None:
                return None
            sum_buf[i, v] = value
            return [send(sum_buf.at[i, v], sum_buf.at[i, v], dev(k)) for k in (1, 2, 3)]

        def side_sum(i, copies):
            if side is None:
                return None
            for copy in copies:
                copy.wait_recv()
            return (sum_buf[i, 0] + sum_buf[i, 1]) + (sum_buf[i, 2] + sum_buf[i, 3])

        stage[spot] = chunk
        copies = [send(stage.at[spot], stage.at[spot], pdev(i, j)) for i, j in near]
        beside = side_start(0, y, ydev, side)
        for copy in copies:
            copy.wait_recv()
        out[pl.ds(pl.multiple_of(x * BLOCK, BLOCK), BLOCK), :] = stage[...].reshape(BLOCK, WIDTH)

        def piece(v, start, stop):
            return out.at[pl.ds(pl.multiple_of(v * BLOCK + start, 32), stop - start)]

        up, down = ring_gather(piece, (32, 64, 96, 128), x, xdev)
        beside = side_start(1, zl, zdev, side_sum(0, beside))
        for copy in up[2:] + down[2:]:
            copy.wait_recv()
        return side_start(2, x, xdev, side_sum(1, beside)), side_sum

    gather_all(own, gather_y.at[0], feats.at[0])
    centered[...] = (feats[0].astype(F32) - dec_bias[...]).astype(BF16)

    def expand(a, weight):
        def body(n, carry):
            columns = pl.ds(pl.multiple_of(n * STEP, STEP), STEP)
            out = jnp.dot(a[...], weight[:, columns], preferred_element_type=F32)
            for i in range(STEP // BLOCK):
                piece = out[:, i * BLOCK : (i + 1) * BLOCK]
                part[n * (STEP // BLOCK) + i] = piece.reshape(TOKENS // OWN, OWN, BLOCK)
            return carry

        lax.fori_loop(0, LOCAL // STEP, body, 0)

    def reduce_slots(use, finish_tile, between=None):
        low = slots // 2
        psend, precv = pair_send.at[use], pair_recv.at[use]
        rsend, rrecv = ring_send.at[use], ring_recv.at[use]

        def loop(body, start=0, stop=slots):
            def step(c, carry):
                body(c, table[1, c], table[0, c] * 8)
                return carry

            lax.fori_loop(start, stop, step, 0)

        pair = {}
        for ks in ((2,), (1, 3, 0)):

            def to_pair(c, panel, row):
                for k in ks:
                    t = turn(tok, k)
                    psend[t, c] = part[panel, row + (1 - seg) * 4 + t].astype(BF16)

            loop(to_pair)
            for k in ks:
                t = turn(tok, k)
                pair[k] = send(psend.at[t], precv.at[t], sibling)

        def mine(k, c, panel, row):
            t = turn(tok, k)
            return part[panel, row + seg * 4 + t] + precv[t, c].astype(F32)

        pair[2].wait_recv()

        def far(c, panel, row):
            rsend[0, c] = mine(2, c, panel, row).astype(BF16)

        def ring(i, start, stop, k):
            span = pl.ds(start, stop - start)
            return send(rsend.at[i, span], rrecv.at[i, span], tdev(k))

        quarter = low // 2
        lows = ((0, quarter), (quarter, low))
        highs = ((low, low + quarter), (low + quarter, slots))
        first_up, first_down = [], []
        for i in (0, 1):
            loop(far, *lows[i])
            first_up.append(ring(0, *lows[i], 1))
            loop(far, *highs[i])
            first_down.append(ring(0, *highs[i], 3))
        pair[1].wait_recv()

        def near_up(c, panel, row):
            rsend[1, c] = mine(1, c, panel, row).astype(BF16)

        loop(near_up, low, slots)
        rest = [ring(1, low, slots, 1)]
        pair[3].wait_recv()

        def near_down(c, panel, row):
            rsend[2, c] = mine(3, c, panel, row).astype(BF16)

        loop(near_down, 0, low)
        rest.append(ring(2, 0, low, 3))

        def merged_up(c, panel, row):
            rsend[1, c] = (mine(1, c, panel, row) + rrecv[0, c].astype(F32)).astype(BF16)

        def merged_down(c, panel, row):
            rsend[2, c] = (mine(3, c, panel, row) + rrecv[0, c].astype(F32)).astype(BF16)

        for i in (0, 1):
            first_up[i].wait_recv()
            loop(merged_up, *lows[i])
            rest.append(ring(1, *lows[i], 1))
            first_down[i].wait_recv()
            loop(merged_down, *highs[i])
            rest.append(ring(2, *highs[i], 3))
        pair[0].wait_recv()
        if between is not None:
            between()
        for copy in rest:
            copy.wait_recv()
        all_tiles = gathered.at[use]

        def last(c, panel, row):
            total = mine(0, c, panel, row) + rrecv[1, c].astype(F32) + rrecv[2, c].astype(F32)
            all_tiles[me, c] = finish_tile(c, panel, total).astype(BF16)

        loop(last)

        def piece(v, start, stop):
            return all_tiles.at[seg * 4 + v, pl.ds(start, stop - start)]

        def whole(v):
            return all_tiles.at[seg * 4 + v]

        crossing = [send(whole(tok), whole(tok), sibling)]
        up, down = ring_gather(piece, (quarter, low, low + quarter, slots), tok, tdev)
        up[2].wait_recv()
        before = turn(tok, 3)
        crossing.append(send(whole(before), whole(before), sibling))
        down[2].wait_recv()
        after = turn(tok, 1)
        crossing.append(send(whole(after), whole(after), sibling))
        for copy in up[3:] + down[3:]:
            copy.wait_recv()
        far_side = turn(tok, 2)
        crossing.append(send(whole(far_side), whole(far_side), sibling))
        for copy in crossing:
            copy.wait_recv()

        def spread(b, carry):
            for p in range(PANELS):
                slot = table[2, b * PANELS + p]
                active = table[3, b * PANELS + p] > 0
                for j in range(8):
                    tile = all_tiles[j, slot]
                    at = pl.multiple_of(b * BLOCK + j * OWN, OWN)
                    dense[use, pl.ds(at, OWN), p * BLOCK : (p + 1) * BLOCK] = jnp.where(
                        active, tile, jnp.zeros_like(tile)
                    )
            return carry

        lax.fori_loop(0, BLOCKS, spread, 0)

    expand(centered, enc_w)

    def latents_of(c, panel, total):
        activation, derivative = gelu_pair(total + enc_bias[pl.ds(panel, 1), :])
        slope[c] = derivative
        return activation

    reduce_slots(0, latents_of)

    latents = dense.at[0]

    def decode_block(k):
        b = pl.multiple_of(turn(x, k) * BLOCK, BLOCK)
        return nt(latents[pl.ds(b, BLOCK), :], dec_w[...])

    far = decode_block(2)
    xs_send[0] = far.astype(BF16)
    first_up = send(xs_send.at[0, pl.ds(0, 64)], xs_recv.at[0, pl.ds(0, 64)], xdev(1))
    first_down = send(xs_send.at[0, pl.ds(64, 64)], xs_recv.at[0, pl.ds(64, 64)], xdev(3))

    def decode_near(i, carry):
        k = turn(i, 3)
        decoded[k] = decode_block(k)
        return carry

    lax.fori_loop(0, 3, decode_near, 0)
    part_up = decoded[1]
    xs_send[1, 64:, :] = part_up[64:, :].astype(BF16)
    second_up = send(xs_send.at[1, pl.ds(64, 64)], xs_recv.at[1, pl.ds(64, 64)], xdev(1))
    block_own[0:64, :] = part_up[:64, :]
    part_down = decoded[3]
    xs_send[2, :64, :] = part_down[:64, :].astype(BF16)
    second_down = send(xs_send.at[2, pl.ds(0, 64)], xs_recv.at[2, pl.ds(0, 64)], xdev(3))
    block_own[64:128, :] = part_down[64:, :]
    first_up.wait_recv()
    xs_send[1, :64, :] = (block_own[0:64, :] + xs_recv[0, :64, :].astype(F32)).astype(BF16)
    third_up = send(xs_send.at[1, pl.ds(0, 64)], xs_recv.at[1, pl.ds(0, 64)], xdev(1))
    first_down.wait_recv()
    xs_send[2, 64:, :] = (block_own[64:128, :] + xs_recv[0, 64:, :].astype(F32)).astype(BF16)
    third_down = send(xs_send.at[2, pl.ds(64, 64)], xs_recv.at[2, pl.ds(64, 64)], xdev(3))
    block_own[...] = decoded[0]
    for copy in (second_up, second_down, third_up, third_down):
        copy.wait_recv()
    block_own[...] = block_own[...] + xs_recv[1].astype(F32) + xs_recv[2].astype(F32)

    ps_send[...] = block_own[...].astype(BF16).reshape(16, 8, WIDTH)
    copies = [send(ps_send.at[plane(i, j)], ps_recv.at[spot], pdev(i, j)) for i, j in near]
    rebuilt = block_own[pl.ds(pl.multiple_of(spot * 8, 8), 8), :]
    for copy in copies:
        copy.wait_recv()
    for i, j in near:
        rebuilt = rebuilt + ps_recv[plane(i, j)].astype(F32)

    error = rebuilt + dec_bias[...] - own_rows[...].astype(F32)
    squared = jnp.sum(jnp.sum(error * error, axis=1, keepdims=True), axis=0, keepdims=True)
    beside, side_sum = gather_all(
        error.astype(BF16), gather_y.at[1], feats.at[1], jnp.broadcast_to(squared, (8, 128))
    )
    errors = feats.at[1]
    expand(errors, dec_w)
    sq_buf[1, me] = side_sum(2, beside)
    loss_copies = group_start(sq_buf.at[1])
    store_dec = pltpu.make_async_copy(dec_v, dec_out, local_sem.at[7])
    store_enc = pltpu.make_async_copy(enc_v, enc_out, local_sem.at[8])

    def outer(a, use, result):
        def body(n, carry):
            columns = pl.ds(pl.multiple_of(n * STEP, STEP), STEP)
            result[:, columns] = tn(a[...], dense[use, :, columns]).astype(BF16)
            return carry

        lax.fori_loop(0, LOCAL // STEP, body, 0)

    def decoder_gradient():
        outer(errors, 0, dec_v)
        store_dec.start()
        sq_out[...] = group_sum(sq_buf.at[1], loss_copies) / (TOKENS * D)

    reduce_slots(1, lambda c, panel, total: total * slope[c], decoder_gradient)
    outer(centered, 1, enc_v)
    store_enc.start()
    store_dec.wait()
    store_enc.wait()
    for copy in started:
        copy.wait_send()


def step(place, slots, table, resid_mid, mlp_out, post_gain, enc_weight, enc_bias, dec_weight, dec_bias):
    vmem = pl.BlockSpec(memory_space=pltpu.VMEM)
    hbm = pl.BlockSpec(memory_space=pltpu.HBM)
    low = pltpu.VMEM
    return pl.pallas_call(
        functools.partial(kernel, slots),
        name=f"sae_step_{slots}",
        out_shape=(
            jax.ShapeDtypeStruct((8, 128), F32),
            jax.ShapeDtypeStruct((WIDTH, LOCAL), BF16),
            jax.ShapeDtypeStruct((WIDTH, LOCAL), BF16),
        ),
        in_specs=[pl.BlockSpec(memory_space=pltpu.SMEM)] + [hbm] * 7,
        out_specs=(vmem, hbm, hbm),
        scratch_shapes=[
            low((8, WIDTH), BF16),
            low((8, WIDTH), BF16),
            low((1, WIDTH), F32),
            low((PANELS, BLOCK), F32),
            low((1, WIDTH), F32),
            low((WIDTH, LOCAL), BF16),
            low((WIDTH, LOCAL), BF16),
            low((2, 8, 8, 128), F32),
            low((8, WIDTH), BF16),
            low((2, 16, 8, WIDTH), BF16),
            low((2, TOKENS, WIDTH), BF16),
            low((TOKENS, WIDTH), BF16),
            low((PANELS, TOKENS // OWN, OWN, BLOCK), F32),
            low((2, 4, slots, OWN, BLOCK), BF16),
            low((2, 4, slots, OWN, BLOCK), BF16),
            low((2, 3, slots, OWN, BLOCK), BF16),
            low((2, 3, slots, OWN, BLOCK), BF16),
            low((slots, OWN, BLOCK), F32),
            low((2, 8, slots, OWN, BLOCK), BF16),
            low((2, TOKENS, LOCAL), BF16),
            low((BLOCKS, BLOCK, WIDTH), F32),
            low((BLOCK, WIDTH), F32),
            low((3, BLOCK, WIDTH), BF16),
            low((3, BLOCK, WIDTH), BF16),
            low((16, 8, WIDTH), BF16),
            low((16, 8, WIDTH), BF16),
            low((3, 4, 8, 128), F32),
            low((WIDTH, LOCAL), BF16),
            low((WIDTH, LOCAL), BF16),
            pltpu.SemaphoreType.DMA((COPIES,)),
            pltpu.SemaphoreType.DMA((COPIES,)),
            pltpu.SemaphoreType.DMA((9,)),
        ],
        compiler_params=pltpu.CompilerParams(
            collective_id=place, has_side_effects=True, vmem_limit_bytes=48 * 1024 * 1024
        ),
    )(
        table,
        resid_mid,
        mlp_out,
        post_gain.reshape(1, WIDTH),
        enc_bias.reshape(PANELS, BLOCK),
        dec_bias.reshape(1, WIDTH),
        enc_weight,
        dec_weight.T,
    )


def tables(panel_lists):
    ids = lax.axis_index("lat") * PANELS + jnp.arange(PANELS, dtype=jnp.int32)
    active = jnp.any(panel_lists[:, :, None] == ids[None, None, :], axis=1).reshape(-1)
    active = active.astype(jnp.int32)
    tiles = jnp.arange(BLOCKS * PANELS, dtype=jnp.int32)
    rank = jnp.sum(jnp.where(tiles[None, :] < tiles[:, None], active[None, :], 0), axis=1)
    here = (rank[None, :] == tiles[:, None]) & (active[None, :] > 0)
    tile = jnp.sum(jnp.where(here, tiles[None, :], 0), axis=1)
    slot = jnp.where(active > 0, rank, 0)
    return jnp.stack([tile // PANELS, tile % PANELS, slot, active]).astype(jnp.int32)


def on_device(
    resid_mid, mlp_out, post_gain, enc_weight, enc_bias, dec_weight, dec_bias, panel_lists
):
    table = tables(panel_lists)
    groups = jnp.arange(lax.axis_size("lat"), dtype=jnp.int32)
    per_group = jnp.sum(panel_lists.reshape(1, -1) // PANELS == groups[:, None], axis=1)
    most = jnp.max(per_group)
    loss, enc_grad, dec_grad = lax.switch(
        sum((most > slots).astype(jnp.int32) for slots in CAPACITIES[:-1]),
        [functools.partial(step, i, slots) for i, slots in enumerate(CAPACITIES)],
        table,
        resid_mid,
        mlp_out,
        post_gain,
        enc_weight,
        enc_bias,
        dec_weight,
        dec_bias,
    )
    return loss[0, 0], enc_grad, dec_grad.T


def solution(mesh):
    placed = (
        P("lat", ("segment", "tok")),
        P("lat", ("segment", "tok")),
        P(("segment", "tok")),
        P(("segment", "tok"), "lat"),
        P("lat"),
        P("lat", ("segment", "tok")),
        P(("segment", "tok")),
        P(),
    )
    return jax.shard_map(
        on_device,
        mesh=mesh,
        in_specs=placed,
        out_specs=(P(), P(("segment", "tok"), "lat"), P("lat", ("segment", "tok"))),
        check_vma=False,
    )
```

```python
import functools

import jax
import jax.numpy as jnp
from jax import lax
from jax.experimental import pallas as pl
from jax.experimental.pallas import tpu as pltpu
from jax.sharding import PartitionSpec as P

MESH = pl.DeviceIdType.MESH
D = 4608
TOKENS = 512
WIDTH = 576
LOCAL = 1024
PANELS = 8
BLOCKS = 4
BLOCK = 128
OWN = 16
STEP = 256
F32 = jnp.float32
BF16 = jnp.bfloat16
COPIES = 192
CAPACITIES = (16, 18, 20, 24, 32)


def gelu_pair(x):
    k = 0.7978845608028654
    x2 = x * x
    t = jnp.tanh(k * (x + 0.044715 * (x2 * x)))
    half = 0.5 * (1.0 + t)
    slope = half + (0.5 * x * (1.0 - t * t)) * (k * (1.0 + 0.134145 * x2))
    return x * half, slope


def nt(a, b):
    return lax.dot_general(a, b, (((1,), (1,)), ((), ())), preferred_element_type=F32)


def tn(a, b):
    return lax.dot_general(a, b, (((0,), (0,)), ((), ())), preferred_element_type=F32)


def kernel(
    slots,
    table,
    resid_hbm,
    mlp_hbm,
    gain_hbm,
    enc_bias_hbm,
    dec_bias_hbm,
    enc_w_hbm,
    dec_w_hbm,
    sq_out,
    enc_out,
    dec_out,
    resid,
    mlp,
    gain,
    enc_bias,
    dec_bias,
    enc_w,
    dec_w,
    sq_buf,
    own_rows,
    gather_y,
    feats,
    centered,
    part,
    pair_send,
    pair_recv,
    ring_send,
    ring_recv,
    slope,
    gathered,
    dense,
    decoded,
    block_own,
    xs_send,
    xs_recv,
    ps_send,
    ps_recv,
    sum_buf,
    enc_v,
    dec_v,
    send_sem,
    recv_sem,
    local_sem,
):
    seg = lax.axis_index("segment")
    lat = lax.axis_index("lat")
    tok = lax.axis_index("tok")
    x = lax.div(lat, 16)
    zl = lax.rem(lax.div(lat, 4), 4)
    y = lax.rem(lat, 4)

    def turn(v, k):
        return lax.rem(v + k, 4)

    def xdev(k):
        return (seg, turn(x, k) * 16 + zl * 4 + y, tok)

    def plane(i, j):
        return turn(zl, i) * 4 + turn(y, j)

    near = [(i, j) for i in range(4) for j in range(4) if i or j]
    spot = zl * 4 + y

    def ydev(k):
        return pdev(0, k)

    def zdev(k):
        return pdev(k, 0)

    def pdev(i, j):
        return (seg, x * 16 + plane(i, j), tok)

    def tdev(k):
        return (seg, lat, turn(tok, k))

    sibling = (1 - seg, lat, tok)
    group = [sibling] + [(s, lat, turn(tok, k)) for k in (1, 2, 3) for s in (seg, 1 - seg)]

    counter = [0]
    started = []

    def send(src, dst, device):
        i = counter[0]
        counter[0] += 1
        copy = pltpu.make_async_remote_copy(
            src_ref=src,
            dst_ref=dst,
            send_sem=send_sem.at[i],
            recv_sem=recv_sem.at[i],
            device_id=device,
            device_id_type=MESH,
        )
        copy.start()
        started.append(copy)
        return copy

    loads = [
        pltpu.make_async_copy(src, dst, local_sem.at[i])
        for i, (src, dst) in enumerate(
            (
                (mlp_hbm, mlp),
                (resid_hbm, resid),
                (gain_hbm, gain.at[0]),
                (enc_bias_hbm, enc_bias),
                (dec_bias_hbm, dec_bias.at[0]),
                (enc_w_hbm, enc_w),
                (dec_w_hbm, dec_w),
            )
        )
    ]
    for load in loads:
        load.start()

    barrier = pltpu.get_barrier_semaphore()
    peers = group + [xdev(k) for k in (1, 2, 3)] + [pdev(i, j) for i, j in near]
    for peer in peers:
        pl.semaphore_signal(barrier, inc=1, device_id=peer, device_id_type=MESH)

    loads[0].wait()
    rows = mlp[...].astype(F32)
    me = seg * 4 + tok
    sq_buf[0, me] = jnp.broadcast_to(jnp.sum(rows * rows, axis=1, keepdims=True), (8, 128))
    pl.semaphore_wait(barrier, len(peers))
    for load in loads[1:7]:
        load.wait()

    def group_start(buf):
        return [send(buf.at[me], buf.at[me], peer) for peer in group]

    def group_sum(buf, copies):
        for copy in copies:
            copy.wait_recv()
        total = buf[0]
        for i in range(1, 8):
            total = total + buf[i]
        return total

    squares = group_sum(sq_buf.at[0], group_start(sq_buf.at[0]))[:, :1]
    scale = lax.rsqrt(squares / D + 1e-06)
    own = (resid[...].astype(F32) + rows * scale * gain[...]).astype(BF16)
    own_rows[...] = own

    def ring_gather(piece, cuts, v, dev):
        a, b, c, d = cuts

        def pass_on(owner, start, stop, k):
            ref = piece(owner, start, stop)
            return send(ref, ref, dev(k))

        up = [pass_on(v, 0, a, 1), pass_on(v, a, b, 1)]
        down = [pass_on(v, b, c, 3), pass_on(v, c, d, 3)]
        up.append(pass_on(v, b, d, 1))
        down.append(pass_on(v, 0, b, 3))
        before, after = turn(v, 3), turn(v, 1)
        for i, low, high in ((0, (0, a), (b, c)), (1, (a, b), (c, d))):
            up[i].wait_recv()
            up.append(pass_on(before, *low, 1))
            down[i].wait_recv()
            down.append(pass_on(after, *high, 3))
        return up, down

    def gather_all(chunk, stage, out, side=None):
        def side_start(i, v, dev, value):
            if side is None:
                return None
            sum_buf[i, v] = value
            return [send(sum_buf.at[i, v], sum_buf.at[i, v], dev(k)) for k in (1, 2, 3)]

        def side_sum(i, copies):
            if side is None:
                return None
            for copy in copies:
                copy.wait_recv()
            return (sum_buf[i, 0] + sum_buf[i, 1]) + (sum_buf[i, 2] + sum_buf[i, 3])

        stage[spot] = chunk
        copies = [send(stage.at[spot], stage.at[spot], pdev(i, j)) for i, j in near]
        beside = side_start(0, y, ydev, side)
        for copy in copies:
            copy.wait_recv()
        out[pl.ds(pl.multiple_of(x * BLOCK, BLOCK), BLOCK), :] = stage[...].reshape(BLOCK, WIDTH)

        def piece(v, start, stop):
            return out.at[pl.ds(pl.multiple_of(v * BLOCK + start, 32), stop - start)]

        up, down = ring_gather(piece, (32, 64, 96, 128), x, xdev)
        beside = side_start(1, zl, zdev, side_sum(0, beside))
        for copy in up[2:] + down[2:]:
            copy.wait_recv()
        return side_start(2, x, xdev, side_sum(1, beside)), side_sum

    gather_all(own, gather_y.at[0], feats.at[0])
    centered[...] = (feats[0].astype(F32) - dec_bias[...]).astype(BF16)

    def expand(a, weight):
        def body(n, carry):
            columns = pl.ds(pl.multiple_of(n * STEP, STEP), STEP)
            out = jnp.dot(a[...], weight[:, columns], preferred_element_type=F32)
            for i in range(STEP // BLOCK):
                piece = out[:, i * BLOCK : (i + 1) * BLOCK]
                part[n * (STEP // BLOCK) + i] = piece.reshape(TOKENS // OWN, OWN, BLOCK)
            return carry

        lax.fori_loop(0, LOCAL // STEP, body, 0)

    def reduce_slots(use, finish_tile, between=None):
        low = slots // 2
        psend, precv = pair_send.at[use], pair_recv.at[use]
        rsend, rrecv = ring_send.at[use], ring_recv.at[use]

        def loop(body, start=0, stop=slots):
            def step(c, carry):
                body(c, table[1, c], table[0, c] * 8)
                return carry

            lax.fori_loop(start, stop, step, 0)

        pair = {}
        for ks in ((2,), (1, 3, 0)):

            def to_pair(c, panel, row):
                for k in ks:
                    t = turn(tok, k)
                    psend[t, c] = part[panel, row + (1 - seg) * 4 + t].astype(BF16)

            loop(to_pair)
            for k in ks:
                t = turn(tok, k)
                pair[k] = send(psend.at[t], precv.at[t], sibling)

        def mine(k, c, panel, row):
            t = turn(tok, k)
            return part[panel, row + seg * 4 + t] + precv[t, c].astype(F32)

        pair[2].wait_recv()

        def far(c, panel, row):
            rsend[0, c] = mine(2, c, panel, row).astype(BF16)

        def ring(i, start, stop, k):
            span = pl.ds(start, stop - start)
            return send(rsend.at[i, span], rrecv.at[i, span], tdev(k))

        quarter = low // 2
        lows = ((0, quarter), (quarter, low))
        highs = ((low, low + quarter), (low + quarter, slots))
        first_up, first_down = [], []
        for i in (0, 1):
            loop(far, *lows[i])
            first_up.append(ring(0, *lows[i], 1))
            loop(far, *highs[i])
            first_down.append(ring(0, *highs[i], 3))
        pair[1].wait_recv()

        def near_up(c, panel, row):
            rsend[1, c] = mine(1, c, panel, row).astype(BF16)

        loop(near_up, low, slots)
        rest = [ring(1, low, slots, 1)]
        pair[3].wait_recv()

        def near_down(c, panel, row):
            rsend[2, c] = mine(3, c, panel, row).astype(BF16)

        loop(near_down, 0, low)
        rest.append(ring(2, 0, low, 3))

        def merged_up(c, panel, row):
            rsend[1, c] = (mine(1, c, panel, row) + rrecv[0, c].astype(F32)).astype(BF16)

        def merged_down(c, panel, row):
            rsend[2, c] = (mine(3, c, panel, row) + rrecv[0, c].astype(F32)).astype(BF16)

        for i in (0, 1):
            first_up[i].wait_recv()
            loop(merged_up, *lows[i])
            rest.append(ring(1, *lows[i], 1))
            first_down[i].wait_recv()
            loop(merged_down, *highs[i])
            rest.append(ring(2, *highs[i], 3))
        pair[0].wait_recv()
        if between is not None:
            between()
        for copy in rest:
            copy.wait_recv()
        all_tiles = gathered.at[use]

        def last(c, panel, row):
            total = mine(0, c, panel, row) + rrecv[1, c].astype(F32) + rrecv[2, c].astype(F32)
            all_tiles[me, c] = finish_tile(c, panel, total).astype(BF16)

        loop(last)

        def piece(v, start, stop):
            return all_tiles.at[seg * 4 + v, pl.ds(start, stop - start)]

        def whole(v):
            return all_tiles.at[seg * 4 + v]

        crossing = [send(whole(tok), whole(tok), sibling)]
        up, down = ring_gather(piece, (quarter, low, low + quarter, slots), tok, tdev)
        up[2].wait_recv()
        before = turn(tok, 3)
        crossing.append(send(whole(before), whole(before), sibling))
        down[2].wait_recv()
        after = turn(tok, 1)
        crossing.append(send(whole(after), whole(after), sibling))
        for copy in up[3:] + down[3:]:
            copy.wait_recv()
        far_side = turn(tok, 2)
        crossing.append(send(whole(far_side), whole(far_side), sibling))
        for copy in crossing:
            copy.wait_recv()

        def spread(b, carry):
            for p in range(PANELS):
                slot = table[2, b * PANELS + p]
                active = table[3, b * PANELS + p] > 0
                for j in range(8):
                    tile = all_tiles[j, slot]
                    at = pl.multiple_of(b * BLOCK + j * OWN, OWN)
                    dense[use, pl.ds(at, OWN), p * BLOCK : (p + 1) * BLOCK] = jnp.where(
                        active, tile, jnp.zeros_like(tile)
                    )
            return carry

        lax.fori_loop(0, BLOCKS, spread, 0)

    expand(centered, enc_w)

    def latents_of(c, panel, total):
        activation, derivative = gelu_pair(total + enc_bias[pl.ds(panel, 1), :])
        slope[c] = derivative
        return activation

    reduce_slots(0, latents_of)

    latents = dense.at[0]

    def decode_block(k):
        b = pl.multiple_of(turn(x, k) * BLOCK, BLOCK)
        return nt(latents[pl.ds(b, BLOCK), :], dec_w[...])

    far = decode_block(2)
    xs_send[0] = far.astype(BF16)
    first_up = send(xs_send.at[0, pl.ds(0, 64)], xs_recv.at[0, pl.ds(0, 64)], xdev(1))
    first_down = send(xs_send.at[0, pl.ds(64, 64)], xs_recv.at[0, pl.ds(64, 64)], xdev(3))

    def decode_near(i, carry):
        k = turn(i, 3)
        decoded[k] = decode_block(k)
        return carry

    lax.fori_loop(0, 3, decode_near, 0)
    part_up = decoded[1]
    xs_send[1, 64:, :] = part_up[64:, :].astype(BF16)
    second_up = send(xs_send.at[1, pl.ds(64, 64)], xs_recv.at[1, pl.ds(64, 64)], xdev(1))
    block_own[0:64, :] = part_up[:64, :]
    part_down = decoded[3]
    xs_send[2, :64, :] = part_down[:64, :].astype(BF16)
    second_down = send(xs_send.at[2, pl.ds(0, 64)], xs_recv.at[2, pl.ds(0, 64)], xdev(3))
    block_own[64:128, :] = part_down[64:, :]
    first_up.wait_recv()
    xs_send[1, :64, :] = (block_own[0:64, :] + xs_recv[0, :64, :].astype(F32)).astype(BF16)
    third_up = send(xs_send.at[1, pl.ds(0, 64)], xs_recv.at[1, pl.ds(0, 64)], xdev(1))
    first_down.wait_recv()
    xs_send[2, 64:, :] = (block_own[64:128, :] + xs_recv[0, 64:, :].astype(F32)).astype(BF16)
    third_down = send(xs_send.at[2, pl.ds(64, 64)], xs_recv.at[2, pl.ds(64, 64)], xdev(3))
    block_own[...] = decoded[0]
    for copy in (second_up, second_down, third_up, third_down):
        copy.wait_recv()
    block_own[...] = block_own[...] + xs_recv[1].astype(F32) + xs_recv[2].astype(F32)

    ps_send[...] = block_own[...].astype(BF16).reshape(16, 8, WIDTH)
    copies = [send(ps_send.at[plane(i, j)], ps_recv.at[spot], pdev(i, j)) for i, j in near]
    rebuilt = block_own[pl.ds(pl.multiple_of(spot * 8, 8), 8), :]
    for copy in copies:
        copy.wait_recv()
    for i, j in near:
        rebuilt = rebuilt + ps_recv[plane(i, j)].astype(F32)

    error = rebuilt + dec_bias[...] - own_rows[...].astype(F32)
    squared = jnp.sum(jnp.sum(error * error, axis=1, keepdims=True), axis=0, keepdims=True)
    beside, side_sum = gather_all(
        error.astype(BF16), gather_y.at[1], feats.at[1], jnp.broadcast_to(squared, (8, 128))
    )
    errors = feats.at[1]
    expand(errors, dec_w)
    sq_buf[1, me] = side_sum(2, beside)
    loss_copies = group_start(sq_buf.at[1])
    store_dec = pltpu.make_async_copy(dec_v, dec_out, local_sem.at[7])
    store_enc = pltpu.make_async_copy(enc_v, enc_out, local_sem.at[8])

    def outer(a, use, result):
        def body(n, carry):
            columns = pl.ds(pl.multiple_of(n * STEP, STEP), STEP)
            result[:, columns] = tn(a[...], dense[use, :, columns]).astype(BF16)
            return carry

        lax.fori_loop(0, LOCAL // STEP, body, 0)

    def decoder_gradient():
        outer(errors, 0, dec_v)
        store_dec.start()
        sq_out[...] = group_sum(sq_buf.at[1], loss_copies) / (TOKENS * D)

    reduce_slots(1, lambda c, panel, total: total * slope[c], decoder_gradient)
    outer(centered, 1, enc_v)
    store_enc.start()
    store_dec.wait()
    store_enc.wait()
    for copy in started:
        copy.wait_send()


def step(place, slots, table, resid_mid, mlp_out, post_gain, enc_weight, enc_bias, dec_weight, dec_bias):
    vmem = pl.BlockSpec(memory_space=pltpu.VMEM)
    hbm = pl.BlockSpec(memory_space=pltpu.HBM)
    low = pltpu.VMEM
    return pl.pallas_call(
        functools.partial(kernel, slots),
        name=f"sae_step_{slots}",
        out_shape=(
            jax.ShapeDtypeStruct((8, 128), F32),
            jax.ShapeDtypeStruct((WIDTH, LOCAL), BF16),
            jax.ShapeDtypeStruct((WIDTH, LOCAL), BF16),
        ),
        in_specs=[pl.BlockSpec(memory_space=pltpu.SMEM)] + [hbm] * 7,
        out_specs=(vmem, hbm, hbm),
        scratch_shapes=[
            low((8, WIDTH), BF16),
            low((8, WIDTH), BF16),
            low((1, WIDTH), F32),
            low((PANELS, BLOCK), F32),
            low((1, WIDTH), F32),
            low((WIDTH, LOCAL), BF16),
            low((WIDTH, LOCAL), BF16),
            low((2, 8, 8, 128), F32),
            low((8, WIDTH), BF16),
            low((2, 16, 8, WIDTH), BF16),
            low((2, TOKENS, WIDTH), BF16),
            low((TOKENS, WIDTH), BF16),
            low((PANELS, TOKENS // OWN, OWN, BLOCK), F32),
            low((2, 4, slots, OWN, BLOCK), BF16),
            low((2, 4, slots, OWN, BLOCK), BF16),
            low((2, 3, slots, OWN, BLOCK), BF16),
            low((2, 3, slots, OWN, BLOCK), BF16),
            low((slots, OWN, BLOCK), F32),
            low((2, 8, slots, OWN, BLOCK), BF16),
            low((2, TOKENS, LOCAL), BF16),
            low((BLOCKS, BLOCK, WIDTH), F32),
            low((BLOCK, WIDTH), F32),
            low((3, BLOCK, WIDTH), BF16),
            low((3, BLOCK, WIDTH), BF16),
            low((16, 8, WIDTH), BF16),
            low((16, 8, WIDTH), BF16),
            low((3, 4, 8, 128), F32),
            low((WIDTH, LOCAL), BF16),
            low((WIDTH, LOCAL), BF16),
            pltpu.SemaphoreType.DMA((COPIES,)),
            pltpu.SemaphoreType.DMA((COPIES,)),
            pltpu.SemaphoreType.DMA((9,)),
        ],
        compiler_params=pltpu.CompilerParams(
            collective_id=place, has_side_effects=True, vmem_limit_bytes=48 * 1024 * 1024
        ),
    )(
        table,
        resid_mid,
        mlp_out,
        post_gain,
        enc_bias.reshape(PANELS, BLOCK),
        dec_bias,
        enc_weight,
        dec_weight.T,
    )


def tables(panel_lists):
    ids = lax.axis_index("lat") * PANELS + jnp.arange(PANELS, dtype=jnp.int32)
    active = jnp.any(panel_lists[:, :, None] == ids[None, None, :], axis=1).reshape(-1)
    active = active.astype(jnp.int32)
    tiles = jnp.arange(BLOCKS * PANELS, dtype=jnp.int32)
    rank = jnp.sum(jnp.where(tiles[None, :] < tiles[:, None], active[None, :], 0), axis=1)
    here = (rank[None, :] == tiles[:, None]) & (active[None, :] > 0)
    tile = jnp.sum(jnp.where(here, tiles[None, :], 0), axis=1)
    slot = jnp.where(active > 0, rank, 0)
    return jnp.stack([tile // PANELS, tile % PANELS, slot, active]).astype(jnp.int32)


def on_device(
    resid_mid, mlp_out, post_gain, enc_weight, enc_bias, dec_weight, dec_bias, panel_lists
):
    table = tables(panel_lists)
    groups = jnp.arange(lax.axis_size("lat"), dtype=jnp.int32)
    per_group = jnp.sum(panel_lists.reshape(1, -1) // PANELS == groups[:, None], axis=1)
    most = jnp.max(per_group)
    loss, enc_grad, dec_grad = lax.switch(
        sum((most > slots).astype(jnp.int32) for slots in CAPACITIES[:-1]),
        [functools.partial(step, i, slots) for i, slots in enumerate(CAPACITIES)],
        table,
        resid_mid,
        mlp_out,
        post_gain,
        enc_weight,
        enc_bias,
        dec_weight,
        dec_bias,
    )
    return loss[0, 0], enc_grad, dec_grad.T


def solution(mesh):
    placed = (
        P("lat", ("segment", "tok")),
        P("lat", ("segment", "tok")),
        P(("segment", "tok")),
        P(("segment", "tok"), "lat"),
        P("lat"),
        P("lat", ("segment", "tok")),
        P(("segment", "tok")),
        P(),
    )
    return jax.shard_map(
        on_device,
        mesh=mesh,
        in_specs=placed,
        out_specs=(P(), P(("segment", "tok"), "lat"), P("lat", ("segment", "tok"))),
        check_vma=False,
    )
```
